256 devices in a mesh: dp: 8 (over y, z_hi), row: 4 (over z_lo), col: 8 (over x, core).
Axes of the slice: x: 4, y: 4, z: 8 (z_hi: 2, z_lo: 4; z = z_hi * 4 + z_lo), core: 2. Of those that a mesh axis runs over, the one named last changes fastest.
Arguments:
- tokens: bfloat16 [6144, 4096], P(('dp', 'col'), 'row'), may hold values from -6 to 6
- out_grad: bfloat16 [6144, 4096], P(('dp', 'col'), 'row'), may hold values from -6 to 6
- in_weight: bfloat16 [4096, 14336], P('row', 'col'), may hold values from -0.09375 to 0.09375
- out_weight: bfloat16 [14336, 4096], P('col', 'row'), may hold values from -0.046875 to 0.046875
- active_lists: int32 [48, 64], P('dp'), may hold values from 0 to 111, all different within a row
- active_counts: int32 [48], P('dp'), may hold values from 32 to 64, as said below
Outputs:
- token_grad: bfloat16 [6144, 4096], P(('dp', 'col'), 'row')
- in_weight_grad: bfloat16 [14336, 4096], P(('col', 'dp'), 'row')
- out_weight_grad: bfloat16 [14336, 4096], P(('col', 'dp'), 'row')
The draws below stay inside these ranges and needn't reach their ends.
Inputs may be any that keep to these rules, and one draw needn't show every extreme that they name: `active_lists`: all 64 entries of a row differ; only the first active_counts entries of a row count. `active_counts`: some token block has all 64 entries active.
All inputs are finite; a program needn't handle non-finite values.
Results may differ from the reference program's by a relative error of at most 0.019.
Values may be sent and summed in bfloat16 or wider, within the bound.
No kernel may reach another device: no remote copies, remote signals or barrier semaphores. Data moves between devices by JAX's collectives and lax.ppermute only.
A program may use at most 128 MiB of HBM per device.

```python
import jax
import jax.numpy as jnp
from jax import lax

D = 4096
FF = 14336
BLK = 128
MAXACT = 64
TOKENS = 6144
TB = 48


def draw_active_counts(key, part):
    first, second = jax.random.split(key)
    drawn = jax.random.randint(first, (TB,), MAXACT // 2, MAXACT + 1, dtype=jnp.int32)
    chosen = jax.random.randint(second, (), 0, TB, dtype=jnp.int32)
    return jnp.where(jnp.arange(TB, dtype=jnp.int32) == chosen, MAXACT, drawn).astype(jnp.int32)


def levels(own_key, extent, pieces, least, high):
    level, own = 1.0, jax.random.fold_in(own_key, 6)
    for dim, parts in pieces:
        draws = jnp.exp(jax.random.uniform(jax.random.fold_in(own, dim), (parts,), jnp.float32, least / len(pieces), high / len(pieces)))
        level = level * jnp.repeat(draws, extent[dim] // parts).reshape([-1 if axis == dim else 1 for axis in range(len(extent))])
    return level


def distinct(own_key, rows, number_of, top, lift):
    sequence = jax.random.permutation(jax.random.fold_in(own_key, 1), number_of)
    boost = sequence
    for power in range(3):
        boost = boost * boost // number_of
    boost = boost * lift // number_of
    tickets = jax.random.randint(jax.random.fold_in(own_key, 2), (rows, number_of), 0, 4096) + boost
    fixed_rows = jax.random.permutation(jax.random.fold_in(own_key, 3), rows)[jnp.arange(number_of) % rows]
    tickets = jnp.where(jnp.arange(rows)[:, None] == fixed_rows[None, :], 1 << 14, tickets)
    merit = tickets * number_of + jnp.arange(number_of)
    return lax.top_k(merit.astype(jnp.int32), top)[1].astype(jnp.int32)


def centred(own_key, extent, scale, limit, cuts=(), kind=jnp.bfloat16):
    values = jax.random.normal(own_key, extent, jnp.float32) * scale
    if len(cuts) > 0:
        values = levels(own_key, extent, cuts, -0.22, 0.18) * values
    return jnp.clip(values, min=-limit, max=limit).astype(kind)


def setup_inputs(seed: int = 0) -> dict:
    key_of = jax.random.split(jax.random.key(seed), 7)
    tokens = centred(key_of[0], (TOKENS, D), 1.0, 6.0, ((0, 64), (1, 4)))
    out_grad = centred(key_of[1], (TOKENS, D), 1.0, 6.0, ((0, 64), (1, 4)))
    in_weight = centred(key_of[2], (D, FF), D ** -0.5, 0.09375, ((0, 4), (1, 8)))
    out_weight = centred(key_of[3], (FF, D), FF ** -0.5, 0.046875, ((0, 8), (1, 4)))
    active_lists = distinct(key_of[4], TB, FF // BLK, MAXACT, 4681)
    active_counts = draw_active_counts(jax.random.fold_in(key_of[6], 71), 0)
    return dict(tokens=tokens, out_grad=out_grad, in_weight=in_weight, out_weight=out_weight, active_lists=active_lists, active_counts=active_counts)


def reference(tokens, out_grad, in_weight, out_weight, active_lists, active_counts):
    blocks = FF // BLK
    slots = jnp.arange(MAXACT, dtype=jnp.int32)
    valid = slots[None, :] < active_counts[:, None]
    wanted = jnp.arange(blocks, dtype=jnp.int32)
    hits = (active_lists[:, :, None] == wanted[None, None, :]) & valid[:, :, None]
    block_mask = jnp.any(hits, axis=1).astype(jnp.float32)
    row_mask = jnp.repeat(block_mask, BLK, axis=0)
    pre = jnp.dot(tokens, in_weight, preferred_element_type=jnp.float32)
    back = lax.dot_general(out_grad, out_weight, (((1,), (1,)), ((), ())), preferred_element_type=jnp.float32)
    lifted = jax.nn.relu(pre).reshape(TOKENS, blocks, BLK) * row_mask[:, :, None]
    hidden = (lifted * lifted).reshape(TOKENS, FF).astype(jnp.bfloat16)
    hidden_grad = (back.reshape(TOKENS, blocks, BLK) * (2.0 * lifted)).reshape(TOKENS, FF).astype(jnp.bfloat16)
    token_grad = lax.dot_general(hidden_grad, in_weight, (((1,), (1,)), ((), ())), preferred_element_type=jnp.float32)
    scale = TOKENS ** -0.5
    out_weight_grad = lax.dot_general(hidden, out_grad, (((0,), (0,)), ((), ())), preferred_element_type=jnp.float32) * scale
    in_weight_grad = lax.dot_general(hidden_grad, tokens, (((0,), (0,)), ((), ())), preferred_element_type=jnp.float32) * scale
    return (token_grad.astype(jnp.bfloat16), in_weight_grad.astype(jnp.bfloat16), out_weight_grad.astype(jnp.bfloat16))
```

```python
import functools

import jax
import jax.numpy as jnp
from jax import lax
from jax.experimental import pallas as pl
from jax.experimental.pallas import tpu as pltpu
from jax.sharding import PartitionSpec as P

BLK = 128
F32 = jnp.float32
BF16 = jnp.bfloat16
X_SHIFT = {s: [(c, ((c // 2 + s) % 4) * 2 + c % 2) for c in range(8)] for s in (1, 2, 3)}
CORE_SWAP = [(c, c ^ 1) for c in range(8)]
Y_SHIFT = {s: [(d, ((d // 2 + s) % 4) * 2 + d % 2) for d in range(8)] for s in (1, 3)}
HALF_SWAP = [(d, d ^ 1) for d in range(8)]
ROWS = 4


def pick(stack, index):
    return lax.dynamic_index_in_dim(stack, index, 0, keepdims=False)


def add(*terms):
    total = terms[0].astype(F32)
    for term in terms[1:]:
        total = total + term.astype(F32)
    return total


def make_slots(active_lists, active_counts, first_block, local_blocks, capacity):
    slots = jnp.arange(active_lists.shape[1], dtype=jnp.int32)
    valid = slots[None, :] < active_counts[:, None]
    wanted = first_block + jnp.arange(local_blocks, dtype=jnp.int32)
    hits = (active_lists[:, :, None] == wanted[None, None, :]) & valid[:, :, None]
    active = jnp.any(hits, axis=1).astype(jnp.int32).reshape(-1)
    pairs = jnp.arange(active.shape[0], dtype=jnp.int32)
    before = jnp.sum(jnp.where(pairs[None, :] < pairs[:, None], active[None, :], 0), axis=1)
    place = jnp.where(active > 0, before, -1)
    want = jnp.arange(capacity, dtype=jnp.int32)
    pair = jnp.sum(jnp.where(place[None, :] == want[:, None], pairs[None, :], 0), axis=1)
    return pair, jnp.sum(active)


def project_kernel(rhs_dims, blocks, pair_ref, x_ref, w_ref, out_ref, dense_ref):
    wide = 2 * BLK
    for n in range(blocks // 2):
        cols = slice(n * wide, (n + 1) * wide)
        w = w_ref[:, cols] if rhs_dims == 0 else w_ref[cols, :]
        dense_ref[:, cols] = lax.dot_general(
            x_ref[...], w, (((1,), (rhs_dims,)), ((), ())), preferred_element_type=F32
        ).astype(BF16)

    def one(j, carry):
        pair = pair_ref[j]
        t = pl.multiple_of((pair // blocks) * BLK, BLK)
        f = pl.multiple_of((pair % blocks) * BLK, BLK)
        out_ref[pl.ds(pl.multiple_of(j * BLK, BLK), BLK), :] = dense_ref[pl.ds(t, BLK), pl.ds(f, BLK)]
        return carry

    lax.fori_loop(0, out_ref.shape[0] // BLK, one, 0)


def project(pair, x, w, rhs_dims):
    height, depth = x.shape
    width = w.shape[1 - rhs_dims]
    slots = pair.shape[0]
    return pl.pallas_call(
        functools.partial(project_kernel, rhs_dims, width // BLK),
        out_shape=jax.ShapeDtypeStruct((slots * BLK, BLK), BF16),
        in_specs=[
            pl.BlockSpec(memory_space=pltpu.SMEM),
            pl.BlockSpec(memory_space=pltpu.VMEM),
            pl.BlockSpec(memory_space=pltpu.VMEM),
        ],
        out_specs=pl.BlockSpec(memory_space=pltpu.VMEM),
        scratch_shapes=[pltpu.VMEM((height, width), BF16)],
        compiler_params=pltpu.CompilerParams(vmem_limit_bytes=24 << 20),
        cost_estimate=pl.CostEstimate(
            flops=2 * height * depth * width,
            bytes_accessed=2 * (height * depth + depth * width + slots * BLK * BLK),
            transcendentals=0,
        ),
    )(pair, x, w)


def spread_kernel(blocks, share, pair_ref, info_ref, *refs):
    dense_ref = refs[-1]
    dense_ref[...] = jnp.zeros_like(dense_ref)
    place, count = info_ref[0], info_ref[1]
    for offset, ref in zip(range(1 - ROWS, ROWS), refs[:-1]):
        owner = place + offset
        first = owner * share
        stop = jnp.where((owner >= 0) & (owner < ROWS), jnp.clip(count - first, 0, share), 0)

        def one(j, carry, ref=ref, first=first):
            pair = pair_ref[first + j]
            t = pl.multiple_of((pair // blocks) * BLK, BLK)
            f = pl.multiple_of((pair % blocks) * BLK, BLK)
            dense_ref[pl.ds(t, BLK), pl.ds(f, BLK)] = ref[pl.ds(pl.multiple_of(j * BLK, BLK), BLK), :]
            return carry

        lax.fori_loop(0, stop, one, 0)


def spread(pair, info, pieces, height, width):
    share = pair.shape[0] // ROWS
    return pl.pallas_call(
        functools.partial(spread_kernel, width // BLK, share),
        out_shape=jax.ShapeDtypeStruct((height, width), BF16),
        in_specs=[pl.BlockSpec(memory_space=pltpu.SMEM)] * 2
        + [pl.BlockSpec(memory_space=pltpu.VMEM)] * len(pieces),
        out_specs=pl.BlockSpec(memory_space=pltpu.VMEM),
        compiler_params=pltpu.CompilerParams(vmem_limit_bytes=24 << 20),
        cost_estimate=pl.CostEstimate(flops=0, bytes_accessed=8 * height * width, transcendentals=0),
    )(pair, info, *pieces)


def gather_col(part, x, core):
    behind = lax.ppermute(part, "col", X_SHIFT[1])
    ahead = lax.ppermute(part, "col", X_SHIFT[3])
    far = lax.ppermute(part, "col", X_SHIFT[2])
    ring = jnp.stack([part, ahead, far, behind, part, ahead, far, behind])
    mine = lax.dynamic_slice_in_dim(ring, (4 - x) % 4, 4, 0)
    other = lax.ppermute(mine, "col", CORE_SWAP)
    both = jnp.where(core == 0, jnp.stack([mine, other], 1), jnp.stack([other, mine], 1))
    return both.reshape(8 * part.shape[0], part.shape[1])


def scatter_row(compact, z):
    quarters = compact.reshape(ROWS, -1, BLK)
    sums = [pick(quarters, z)]
    for sign in (1, -1):
        got = None
        for step in range(1, ROWS):
            index = z + 4 - step if sign > 0 else z - 4 + step
            send = pick(quarters, jnp.clip(index, 0, ROWS - 1))
            if got is not None:
                send = add(send, got).astype(BF16)
            line = range(step) if sign > 0 else range(ROWS - 1, ROWS - 1 - step, -1)
            got = lax.ppermute(send, "row", [(i, i + sign) for i in line])
        sums.append(got)
    return add(*sums)


def gather_row(own):
    below, above = [], []
    for sign, got in ((1, below), (-1, above)):
        send = own
        for step in range(1, ROWS):
            line = range(step - 1, ROWS - 1) if sign > 0 else range(ROWS - step, 0, -1)
            send = lax.ppermute(send, "row", [(i, i + sign) for i in line])
            got.append(send)
    return below[::-1] + [own] + above


def scatter_ring(stack, i, axis, forward, backward):
    rows = stack.shape[1] // 2
    far = pick(stack, (i + 2) % 4)
    first = lax.ppermute(far[:rows], axis, forward)
    second = lax.ppermute(far[rows:], axis, backward)
    right = pick(stack, (i + 1) % 4)
    left = pick(stack, (i + 3) % 4)
    right = jnp.concatenate([add(right[:rows], first).astype(BF16), right[rows:]])
    left = jnp.concatenate([left[:rows], add(left[rows:], second).astype(BF16)])
    return add(
        pick(stack, i), lax.ppermute(right, axis, forward), lax.ppermute(left, axis, backward)
    )


def scatter_dp(term, y, half, scale):
    stack = term.reshape(4, term.shape[0] // 4, term.shape[1])
    part = scatter_ring(stack, y, "dp", Y_SHIFT[1], Y_SHIFT[3])
    halves = part.reshape(2, part.shape[0] // 2, part.shape[1])
    got = lax.ppermute(pick(halves, 1 - half).astype(BF16), "dp", HALF_SWAP)
    return (add(pick(halves, half), got) * scale).astype(BF16)


def scatter_col(term, x, core):
    stack = term.reshape(4, 2, term.shape[0] // 8, term.shape[1])
    keep = lax.dynamic_index_in_dim(stack, core, 1, keepdims=False)
    give = lax.dynamic_index_in_dim(stack, 1 - core, 1, keepdims=False)
    chip = add(keep, lax.ppermute(give, "col", CORE_SWAP)).astype(BF16)
    return scatter_ring(chip, x, "col", X_SHIFT[1], X_SHIFT[3]).astype(BF16)


def contract(lhs, rhs, left, right):
    return lax.dot_general(
        lhs, rhs, (((left,), (right,)), ((), ())), preferred_element_type=F32
    ).astype(BF16)


def run(capacity, tokens, out_grad, in_weight, out_weight, active_lists, active_counts):
    dp, z, col = lax.axis_index("dp"), lax.axis_index("row"), lax.axis_index("col")
    y, half, x, core = dp // 2, dp % 2, col // 2, col % 2
    hidden_local = in_weight.shape[1]
    local_blocks = hidden_local // BLK
    pair, count = make_slots(active_lists, active_counts, col * local_blocks, local_blocks, capacity)
    info = jnp.stack([z, count]).astype(jnp.int32)

    all_tokens = gather_col(tokens, x, core)
    all_grad = gather_col(out_grad, x, core)
    height = all_tokens.shape[0]
    scale = (height * lax.axis_size("dp")) ** (-0.5)

    pre = scatter_row(project(pair, all_tokens, in_weight, 0), z)
    back = scatter_row(project(pair, all_grad, out_weight, 1), z)
    lifted = jax.nn.relu(pre)
    hidden_grad = (back * (2.0 * lifted)).astype(BF16)
    hidden = (lifted * lifted).astype(BF16)

    hidden_grad = spread(pair, info, gather_row(hidden_grad), height, hidden_local)
    token_grad = scatter_col(contract(hidden_grad, in_weight, 1, 1), x, core)
    in_weight_grad = scatter_dp(contract(hidden_grad, all_tokens, 0, 0), y, half, scale)
    hidden = spread(pair, info, gather_row(hidden), height, hidden_local)
    out_weight_grad = scatter_dp(contract(hidden, all_grad, 0, 0), y, half, scale)
    return (token_grad, in_weight_grad, out_weight_grad)


def body(tokens, out_grad, in_weight, out_weight, active_lists, active_counts):
    pairs = active_lists.shape[0] * (in_weight.shape[1] // BLK)
    return run(pairs, tokens, out_grad, in_weight, out_weight, active_lists, active_counts)


def solution(mesh):
    in_specs = (
        P(("dp", "col"), "row"),
        P(("dp", "col"), "row"),
        P("row", "col"),
        P("col", "row"),
        P("dp", None),
        P("dp"),
    )
    out_specs = (P(("dp", "col"), "row"), P(("col", "dp"), "row"), P(("col", "dp"), "row"))
    return jax.shard_map(body, mesh=mesh, in_specs=in_specs, out_specs=out_specs, check_vma=False)
```

```python
import functools

import jax
import jax.numpy as jnp
from jax import lax
from jax.experimental import pallas as pl
from jax.experimental.pallas import tpu as pltpu
from jax.sharding import PartitionSpec as P

BLK = 128
F32 = jnp.float32
BF16 = jnp.bfloat16
X_SHIFT = {s: [(c, ((c // 2 + s) % 4) * 2 + c % 2) for c in range(8)] for s in (1, 2, 3)}
CORE_SWAP = [(c, c ^ 1) for c in range(8)]
Y_SHIFT = {s: [(d, ((d // 2 + s) % 4) * 2 + d % 2) for d in range(8)] for s in (1, 2, 3)}
HALF_SWAP = [(d, d ^ 1) for d in range(8)]
ROWS = 4
CAPACITIES = (56,)


def pick(stack, index):
    return lax.dynamic_index_in_dim(stack, index, 0, keepdims=False)


def add(*terms):
    total = terms[0].astype(F32)
    for term in terms[1:]:
        total = total + term.astype(F32)
    return total


def after(value, *others):
    return lax.optimization_barrier((value, *others))[0]


def active_pairs(active_lists, active_counts, blocks):
    slots = jnp.arange(active_lists.shape[1], dtype=jnp.int32)
    valid = slots[None, :] < active_counts[:, None]
    wanted = jnp.arange(blocks, dtype=jnp.int32)
    hits = (active_lists[:, :, None] == wanted[None, None, :]) & valid[:, :, None]
    return jnp.any(hits, axis=1).astype(jnp.int32)


def most_pairs(active, local_blocks):
    groups = active.reshape(active.shape[0], -1, local_blocks)
    most = jnp.broadcast_to(jnp.max(jnp.sum(groups, axis=(0, 2))), (8, 128))
    for shift in (Y_SHIFT[1], Y_SHIFT[2], HALF_SWAP):
        most = jnp.maximum(most, lax.ppermute(most, "dp", shift))
    return most[0, 0]


def make_slots(active, capacity):
    active = active.reshape(-1)
    pairs = jnp.arange(active.shape[0], dtype=jnp.int32)
    before = jnp.sum(jnp.where(pairs[None, :] < pairs[:, None], active[None, :], 0), axis=1)
    place = jnp.where(active > 0, before, -1)
    want = jnp.arange(capacity, dtype=jnp.int32)
    pair = jnp.sum(jnp.where(place[None, :] == want[:, None], pairs[None, :], 0), axis=1)
    return pair, jnp.sum(active)


def project_kernel(rhs_dims, blocks, pair_ref, x_ref, w_ref, out_ref, dense_ref):
    wide = 2 * BLK
    for n in range(blocks // 2):
        cols = slice(n * wide, (n + 1) * wide)
        w = w_ref[:, cols] if rhs_dims == 0 else w_ref[cols, :]
        dense_ref[:, cols] = lax.dot_general(
            x_ref[...], w, (((1,), (rhs_dims,)), ((), ())), preferred_element_type=F32
        ).astype(BF16)

    def one(j, carry):
        pair = pair_ref[j]
        t = pl.multiple_of((pair // blocks) * BLK, BLK)
        f = pl.multiple_of((pair % blocks) * BLK, BLK)
        out_ref[pl.ds(pl.multiple_of(j * BLK, BLK), BLK), :] = dense_ref[pl.ds(t, BLK), pl.ds(f, BLK)]
        return carry

    lax.fori_loop(0, out_ref.shape[0] // BLK, one, 0)


def project(pair, x, w, rhs_dims):
    height, depth = x.shape
    width = w.shape[1 - rhs_dims]
    slots = pair.shape[0]
    return pl.pallas_call(
        functools.partial(project_kernel, rhs_dims, width // BLK),
        out_shape=jax.ShapeDtypeStruct((slots * BLK, BLK), BF16),
        in_specs=[
            pl.BlockSpec(memory_space=pltpu.SMEM),
            pl.BlockSpec(memory_space=pltpu.VMEM),
            pl.BlockSpec(memory_space=pltpu.VMEM),
        ],
        out_specs=pl.BlockSpec(memory_space=pltpu.VMEM),
        scratch_shapes=[pltpu.VMEM((height, width), BF16)],
        compiler_params=pltpu.CompilerParams(vmem_limit_bytes=24 << 20),
        cost_estimate=pl.CostEstimate(
            flops=2 * height * depth * width,
            bytes_accessed=2 * (height * depth + depth * width + slots * BLK * BLK),
            transcendentals=0,
        ),
    )(pair, x, w)


def spread_kernel(blocks, share, pair_ref, info_ref, *refs):
    dense_ref = refs[-1]
    dense_ref[...] = jnp.zeros_like(dense_ref)
    place, count = info_ref[0], info_ref[1]
    for offset, ref in zip(range(1 - ROWS, ROWS), refs[:-1]):
        owner = place + offset
        first = owner * share
        stop = jnp.where((owner >= 0) & (owner < ROWS), jnp.clip(count - first, 0, share), 0)

        def one(j, carry, ref=ref, first=first):
            pair = pair_ref[first + j]
            t = pl.multiple_of((pair // blocks) * BLK, BLK)
            f = pl.multiple_of((pair % blocks) * BLK, BLK)
            dense_ref[pl.ds(t, BLK), pl.ds(f, BLK)] = ref[pl.ds(pl.multiple_of(j * BLK, BLK), BLK), :]
            return carry

        lax.fori_loop(0, stop, one, 0)


def spread(pair, info, pieces, height, width):
    share = pair.shape[0] // ROWS
    return pl.pallas_call(
        functools.partial(spread_kernel, width // BLK, share),
        out_shape=jax.ShapeDtypeStruct((height, width), BF16),
        in_specs=[pl.BlockSpec(memory_space=pltpu.SMEM)] * 2
        + [pl.BlockSpec(memory_space=pltpu.VMEM)] * len(pieces),
        out_specs=pl.BlockSpec(memory_space=pltpu.VMEM),
        compiler_params=pltpu.CompilerParams(vmem_limit_bytes=24 << 20),
        cost_estimate=pl.CostEstimate(flops=0, bytes_accessed=8 * height * width, transcendentals=0),
    )(pair, info, *pieces)


def gather_col(part, x, core):
    behind = lax.ppermute(part, "col", X_SHIFT[1])
    ahead = lax.ppermute(part, "col", X_SHIFT[3])
    far = lax.ppermute(part, "col", X_SHIFT[2])
    ring = jnp.stack([part, ahead, far, behind, part, ahead, far, behind])
    mine = lax.dynamic_slice_in_dim(ring, (4 - x) % 4, 4, 0)
    other = lax.ppermute(mine, "col", CORE_SWAP)
    both = jnp.where(core == 0, jnp.stack([mine, other], 1), jnp.stack([other, mine], 1))
    return both.reshape(8 * part.shape[0], part.shape[1])


def scatter_row(compact, z):
    quarters = compact.reshape(ROWS, -1, BLK)
    sums = [pick(quarters, z)]
    for sign in (1, -1):
        got = None
        for step in range(1, ROWS):
            index = z + 4 - step if sign > 0 else z - 4 + step
            send = pick(quarters, jnp.clip(index, 0, ROWS - 1))
            if got is not None:
                send = add(send, got).astype(BF16)
            line = range(step) if sign > 0 else range(ROWS - 1, ROWS - 1 - step, -1)
            got = lax.ppermute(send, "row", [(i, i + sign) for i in line])
        sums.append(got)
    return add(*sums)


def gather_row(own):
    below, above = [], []
    for sign, got in ((1, below), (-1, above)):
        send = own
        for step in range(1, ROWS):
            line = range(step - 1, ROWS - 1) if sign > 0 else range(ROWS - step, 0, -1)
            send = lax.ppermute(send, "row", [(i, i + sign) for i in line])
            got.append(send)
    return below[::-1] + [own] + above


def scatter_ring(stack, i, axis, forward, backward):
    rows = stack.shape[1] // 2
    far = pick(stack, (i + 2) % 4)
    first = lax.ppermute(far[:rows], axis, forward)
    second = lax.ppermute(far[rows:], axis, backward)
    right = pick(stack, (i + 1) % 4)
    left = pick(stack, (i + 3) % 4)
    right = jnp.concatenate([add(right[:rows], first).astype(BF16), right[rows:]])
    left = jnp.concatenate([left[:rows], add(left[rows:], second).astype(BF16)])
    return add(
        pick(stack, i), lax.ppermute(right, axis, forward), lax.ppermute(left, axis, backward)
    )


def scatter_y(term, y):
    stack = term.reshape(4, term.shape[0] // 4, term.shape[1])
    return scatter_ring(stack, y, "dp", Y_SHIFT[1], Y_SHIFT[3])


def scatter_half(part, half, scale):
    halves = part.reshape(2, part.shape[0] // 2, part.shape[1])
    got = lax.ppermute(pick(halves, 1 - half).astype(BF16), "dp", HALF_SWAP)
    return (add(pick(halves, half), got) * scale).astype(BF16)


def scatter_col(term, x, core):
    stack = term.reshape(4, 2, term.shape[0] // 8, term.shape[1])
    keep = lax.dynamic_index_in_dim(stack, core, 1, keepdims=False)
    give = lax.dynamic_index_in_dim(stack, 1 - core, 1, keepdims=False)
    chip = add(keep, lax.ppermute(give, "col", CORE_SWAP)).astype(BF16)
    return scatter_ring(chip, x, "col", X_SHIFT[1], X_SHIFT[3]).astype(BF16)


def contract(lhs, rhs, left, right):
    return lax.dot_general(
        lhs, rhs, (((left,), (right,)), ((), ())), preferred_element_type=F32
    ).astype(BF16)


def run(capacity, all_tokens, out_grad, in_weight, out_weight, active):
    dp, z, col = lax.axis_index("dp"), lax.axis_index("row"), lax.axis_index("col")
    y, half, x, core = dp // 2, dp % 2, col // 2, col % 2
    hidden_local = in_weight.shape[1]
    pair, count = make_slots(active, capacity)
    info = jnp.stack([z, count]).astype(jnp.int32)

    all_grad = gather_col(out_grad, x, core)
    height = all_tokens.shape[0]
    scale = (height * lax.axis_size("dp")) ** (-0.5)

    pre = scatter_row(project(pair, all_tokens, in_weight, 0), z)
    back = scatter_row(project(pair, all_grad, out_weight, 1), z)
    lifted = jax.nn.relu(pre)
    hidden_grad = (back * (2.0 * lifted)).astype(BF16)
    hidden = (lifted * lifted).astype(BF16)

    grad_pieces = gather_row(hidden_grad)
    pieces = gather_row(after(hidden, grad_pieces[1], grad_pieces[-2]))
    hidden_grad = spread(pair, info, grad_pieces, height, hidden_local)
    in_part = scatter_y(contract(hidden_grad, all_tokens, 0, 0), y)
    token_grad = scatter_col(contract(hidden_grad, in_weight, 1, 1), x, core)
    hidden = spread(pair, info, pieces, height, hidden_local)
    in_weight_grad = scatter_half(after(in_part, pieces[0], pieces[-1]), half, scale)
    width = all_grad.shape[1] // 2
    out_weight_grad = jnp.concatenate(
        [
            scatter_half(scatter_y(contract(hidden, cols, 0, 0), y), half, scale)
            for cols in (all_grad[:, :width], all_grad[:, width:])
        ],
        axis=1,
    )
    return (token_grad, in_weight_grad, out_weight_grad)


def body(tokens, out_grad, in_weight, out_weight, active_lists, active_counts):
    col = lax.axis_index("col")
    local_blocks = in_weight.shape[1] // BLK
    active = active_pairs(active_lists, active_counts, local_blocks * lax.axis_size("col"))
    most = most_pairs(active, local_blocks)
    active = lax.dynamic_slice_in_dim(active, col * local_blocks, local_blocks, 1)
    all_tokens = gather_col(tokens, col // 2, col % 2)
    fits = sum((most > capacity).astype(jnp.int32) for capacity in CAPACITIES)
    branches = [
        functools.partial(run, capacity) for capacity in (*CAPACITIES, active.shape[0] * local_blocks)
    ]
    return lax.switch(fits, branches, all_tokens, out_grad, in_weight, out_weight, active)


def solution(mesh):
    in_specs = (
        P(("dp", "col"), "row"),
        P(("dp", "col"), "row"),
        P("row", "col"),
        P("col", "row"),
        P("dp", None),
        P("dp"),
    )
    out_specs = (P(("dp", "col"), "row"), P(("col", "dp"), "row"), P(("col", "dp"), "row"))
    return jax.shard_map(body, mesh=mesh, in_specs=in_specs, out_specs=out_specs, check_vma=False)
```

```python
import functools

import jax
import jax.numpy as jnp
from jax import lax
from jax.experimental import pallas as pl
from jax.experimental.pallas import tpu as pltpu
from jax.sharding import PartitionSpec as P

BLK = 128
F32 = jnp.float32
BF16 = jnp.bfloat16
X_SHIFT = {s: [(c, ((c // 2 + s) % 4) * 2 + c % 2) for c in range(8)] for s in (1, 2, 3)}
CORE_SWAP = [(c, c ^ 1) for c in range(8)]
Y_SHIFT = {s: [(d, ((d // 2 + s) % 4) * 2 + d % 2) for d in range(8)] for s in (1, 2, 3)}
HALF_SWAP = [(d, d ^ 1) for d in range(8)]
ROWS = 4
CAPACITIES = (56,)


def pick(stack, index):
    return lax.dynamic_index_in_dim(stack, index, 0, keepdims=False)


def add(*terms):
    total = terms[0].astype(F32)
    for term in terms[1:]:
        total = total + term.astype(F32)
    return total


def after(value, *others):
    return lax.optimization_barrier((value, *others))[0]


def active_pairs(active_lists, active_counts, blocks):
    slots = jnp.arange(active_lists.shape[1], dtype=jnp.int32)
    valid = slots[None, :] < active_counts[:, None]
    wanted = jnp.arange(blocks, dtype=jnp.int32)
    hits = (active_lists[:, :, None] == wanted[None, None, :]) & valid[:, :, None]
    return jnp.any(hits, axis=1).astype(jnp.int32)


def most_pairs(active, local_blocks):
    groups = active.reshape(active.shape[0], -1, local_blocks)
    most = jnp.broadcast_to(jnp.max(jnp.sum(groups, axis=(0, 2))), (8, 128))
    for shift in (Y_SHIFT[1], Y_SHIFT[2], HALF_SWAP):
        most = jnp.maximum(most, lax.ppermute(most, "dp", shift))
    return most[0, 0]


def make_slots(active, capacity):
    active = active.reshape(-1)
    pairs = jnp.arange(active.shape[0], dtype=jnp.int32)
    before = jnp.sum(jnp.where(pairs[None, :] < pairs[:, None], active[None, :], 0), axis=1)
    place = jnp.where(active > 0, before, -1)
    want = jnp.arange(capacity, dtype=jnp.int32)
    pair = jnp.sum(jnp.where(place[None, :] == want[:, None], pairs[None, :], 0), axis=1)
    return pair, jnp.sum(active, keepdims=True)


def project_kernel(rhs_dims, blocks, pair_ref, core_ref, mine_ref, other_ref, w_ref, out_ref, x_ref, dense_ref):
    chips, rows = mine_ref.shape[0], mine_ref.shape[1]
    core = core_ref[0]
    for i in range(chips):
        for ref, at in ((mine_ref, 2 * i + core), (other_ref, 2 * i + 1 - core)):
            x_ref[pl.ds(pl.multiple_of(at * rows, rows), rows), :] = ref[i]
    wide = 2 * BLK
    for n in range(blocks // 2):
        cols = slice(n * wide, (n + 1) * wide)
        w = w_ref[:, cols] if rhs_dims == 0 else w_ref[cols, :]
        dense_ref[:, cols] = lax.dot_general(
            x_ref[...], w, (((1,), (rhs_dims,)), ((), ())), preferred_element_type=F32
        ).astype(BF16)

    def one(j, carry):
        pair = pair_ref[j]
        t = pl.multiple_of((pair // blocks) * BLK, BLK)
        f = pl.multiple_of((pair % blocks) * BLK, BLK)
        out_ref[pl.ds(pl.multiple_of(j * BLK, BLK), BLK), :] = dense_ref[pl.ds(t, BLK), pl.ds(f, BLK)]
        return carry

    lax.fori_loop(0, out_ref.shape[0] // BLK, one, 0)


def project(pair, core, mine, other, w, rhs_dims):
    depth = mine.shape[2]
    height = 2 * mine.shape[0] * mine.shape[1]
    width = w.shape[1 - rhs_dims]
    slots = pair.shape[0]
    return pl.pallas_call(
        functools.partial(project_kernel, rhs_dims, width // BLK),
        out_shape=(
            jax.ShapeDtypeStruct((slots * BLK, BLK), BF16),
            jax.ShapeDtypeStruct((height, depth), BF16),
        ),
        in_specs=[pl.BlockSpec(memory_space=pltpu.SMEM)] * 2
        + [pl.BlockSpec(memory_space=pltpu.VMEM)] * 3,
        out_specs=(pl.BlockSpec(memory_space=pltpu.VMEM), pl.BlockSpec(memory_space=pltpu.VMEM)),
        scratch_shapes=[pltpu.VMEM((height, width), BF16)],
        compiler_params=pltpu.CompilerParams(vmem_limit_bytes=24 << 20),
        cost_estimate=pl.CostEstimate(
            flops=2 * height * depth * width,
            bytes_accessed=2 * (height * depth + depth * width + slots * BLK * BLK),
            transcendentals=0,
        ),
    )(pair, core.reshape(1), mine, other, w)


def spread_kernel(blocks, pair_ref, count_ref, compact_ref, dense_ref):
    dense_ref[...] = jnp.zeros_like(dense_ref)

    def one(j, carry):
        pair = pair_ref[j]
        t = pl.multiple_of((pair // blocks) * BLK, BLK)
        f = pl.multiple_of((pair % blocks) * BLK, BLK)
        dense_ref[pl.ds(t, BLK), pl.ds(f, BLK)] = compact_ref[pl.ds(pl.multiple_of(j * BLK, BLK), BLK), :]
        return carry

    lax.fori_loop(0, jnp.minimum(count_ref[0], pair_ref.shape[0]), one, 0)


def spread(pair, count, compact, height, width):
    return pl.pallas_call(
        functools.partial(spread_kernel, width // BLK),
        out_shape=jax.ShapeDtypeStruct((height, width), BF16),
        in_specs=[pl.BlockSpec(memory_space=pltpu.SMEM)] * 2 + [pl.BlockSpec(memory_space=pltpu.VMEM)],
        out_specs=pl.BlockSpec(memory_space=pltpu.VMEM),
        compiler_params=pltpu.CompilerParams(vmem_limit_bytes=24 << 20),
        cost_estimate=pl.CostEstimate(flops=0, bytes_accessed=8 * height * width, transcendentals=0),
    )(pair, count, compact)


def order_kernel(place_ref, *refs):
    for offset, ref in enumerate(refs[:-1]):
        refs[-1][(place_ref[0] + offset) % 4] = ref[...]


def gather_col(part, x, gate=lambda value: value):
    behind = lax.ppermute(part, "col", X_SHIFT[1])
    ahead = lax.ppermute(part, "col", X_SHIFT[3])
    far = lax.ppermute(part, "col", X_SHIFT[2])
    mine = pl.pallas_call(
        order_kernel,
        out_shape=jax.ShapeDtypeStruct((4, *part.shape), part.dtype),
        in_specs=[pl.BlockSpec(memory_space=pltpu.SMEM)] + [pl.BlockSpec(memory_space=pltpu.VMEM)] * 4,
        out_specs=pl.BlockSpec(memory_space=pltpu.VMEM),
        compiler_params=pltpu.CompilerParams(vmem_limit_bytes=8 << 20),
        cost_estimate=pl.CostEstimate(flops=0, bytes_accessed=16 * part.size, transcendentals=0),
    )(gate(x).reshape(1), part, ahead, far, behind)
    return mine, lax.ppermute(mine, "col", CORE_SWAP)


def scatter_row(compact):
    return lax.psum_scatter(compact, "row", scatter_dimension=0, tiled=True)


def gather_row(own):
    return lax.all_gather(own, "row", axis=0, tiled=True)


def scatter_ring(stack, i, axis, forward, backward):
    rows = stack.shape[1] // 2
    far = pick(stack, (i + 2) % 4)
    first = lax.ppermute(far[:rows], axis, forward)
    second = lax.ppermute(far[rows:], axis, backward)
    right = pick(stack, (i + 1) % 4)
    left = pick(stack, (i + 3) % 4)
    right = jnp.concatenate([add(right[:rows], first).astype(BF16), right[rows:]])
    left = jnp.concatenate([left[:rows], add(left[rows:], second).astype(BF16)])
    return add(
        pick(stack, i), lax.ppermute(right, axis, forward), lax.ppermute(left, axis, backward)
    )


def scatter_y(term, y):
    stack = term.reshape(4, term.shape[0] // 4, term.shape[1])
    return scatter_ring(stack, y, "dp", Y_SHIFT[1], Y_SHIFT[3])


def scatter_half(part, half, scale):
    halves = part.reshape(2, part.shape[0] // 2, part.shape[1])
    got = lax.ppermute(pick(halves, 1 - half).astype(BF16), "dp", HALF_SWAP)
    return (add(pick(halves, half), got) * scale).astype(BF16)


def scatter_col(term, x, core):
    stack = term.reshape(4, 2, term.shape[0] // 8, term.shape[1])
    keep = lax.dynamic_index_in_dim(stack, core, 1, keepdims=False)
    give = lax.dynamic_index_in_dim(stack, 1 - core, 1, keepdims=False)
    chip = add(keep, lax.ppermute(give, "col", CORE_SWAP)).astype(BF16)
    return scatter_ring(chip, x, "col", X_SHIFT[1], X_SHIFT[3]).astype(BF16)


def contract(lhs, rhs, left, right):
    return lax.dot_general(
        lhs, rhs, (((left,), (right,)), ((), ())), preferred_element_type=F32
    ).astype(BF16)


def run(capacity, parts, out_grad, in_weight, out_weight, active):
    dp, z, col = lax.axis_index("dp"), lax.axis_index("row"), lax.axis_index("col")
    y, half, x, core = dp // 2, dp % 2, col // 2, col % 2
    hidden_local = in_weight.shape[1]
    pair, count = make_slots(active, capacity)
    width = out_grad.shape[1] // 2

    pre, all_tokens = project(pair, core, *parts, in_weight, 0)
    height = all_tokens.shape[0]
    scale = (height * lax.axis_size("dp")) ** (-0.5)
    parts = gather_col(after(out_grad, pre), x)
    pre = scatter_row(pre)
    back, all_grad = project(pair, core, *parts, out_weight, 1)
    back = scatter_row(back)
    lifted = jax.nn.relu(pre.astype(F32))
    hidden = gather_row((lifted * lifted).astype(BF16))
    hidden_grad = gather_row((back.astype(F32) * (2.0 * lifted)).astype(BF16))

    hidden = spread(pair, count, hidden, height, hidden_local)
    out_part = scatter_y(contract(hidden, all_grad, 0, 0), y)
    out_weight_grad = scatter_half(after(out_part, hidden_grad), half, scale)
    hidden_grad = spread(pair, count, hidden_grad, height, hidden_local)
    in_weight_grad = jnp.concatenate(
        [
            scatter_half(scatter_y(contract(hidden_grad, cols, 0, 0), y), half, scale)
            for cols in (all_tokens[:, :width], all_tokens[:, width:])
        ],
        axis=1,
    )
    token_grad = scatter_col(contract(hidden_grad, in_weight, 1, 1), x, core)
    return (token_grad, in_weight_grad, out_weight_grad)


def body(tokens, out_grad, in_weight, out_weight, active_lists, active_counts):
    col = lax.axis_index("col")
    local_blocks = in_weight.shape[1] // BLK
    active = active_pairs(active_lists, active_counts, local_blocks * lax.axis_size("col"))
    most = most_pairs(active, local_blocks)
    active = lax.dynamic_slice_in_dim(active, col * local_blocks, local_blocks, 1)
    parts = gather_col(tokens, col // 2, lambda value: after(value, most))
    fits = sum((most > capacity).astype(jnp.int32) for capacity in CAPACITIES)
    branches = [
        functools.partial(run, capacity) for capacity in (*CAPACITIES, active.shape[0] * local_blocks)
    ]
    return lax.switch(fits, branches, parts, out_grad, in_weight, out_weight, active)


def solution(mesh):
    in_specs = (
        P(("dp", "col"), "row"),
        P(("dp", "col"), "row"),
        P("row", "col"),
        P("col", "row"),
        P("dp", None),
        P("dp"),
    )
    out_specs = (P(("dp", "col"), "row"), P(("col", "dp"), "row"), P(("col", "dp"), "row"))
    return jax.shard_map(body, mesh=mesh, in_specs=in_specs, out_specs=out_specs, check_vma=False)
```

```python
import functools

import jax
import jax.numpy as jnp
from jax import lax
from jax.experimental import pallas as pl
from jax.experimental.pallas import tpu as pltpu
from jax.sharding import PartitionSpec as P

BLK = 128
F32 = jnp.float32
BF16 = jnp.bfloat16
X_SHIFT = {s: [(c, ((c // 2 + s) % 4) * 2 + c % 2) for c in range(8)] for s in (1, 2, 3)}
CORE_SWAP = [(c, c ^ 1) for c in range(8)]
Y_SHIFT = {s: [(d, ((d // 2 + s) % 4) * 2 + d % 2) for d in range(8)] for s in (1, 2, 3)}
HALF_SWAP = [(d, d ^ 1) for d in range(8)]
ROWS = 4
CAPACITIES = (56,)


def pick(stack, index):
    return lax.dynamic_index_in_dim(stack, index, 0, keepdims=False)


def add(*terms):
    total = terms[0].astype(F32)
    for term in terms[1:]:
        total = total + term.astype(F32)
    return total


def after(value, *others):
    return lax.optimization_barrier((value, *others))[0]


def active_pairs(active_lists, active_counts, blocks):
    slots = jnp.arange(active_lists.shape[1], dtype=jnp.int32)
    valid = slots[None, :] < active_counts[:, None]
    wanted = jnp.arange(blocks, dtype=jnp.int32)
    hits = (active_lists[:, :, None] == wanted[None, None, :]) & valid[:, :, None]
    return jnp.any(hits, axis=1).astype(jnp.int32)


def most_pairs(active, local_blocks):
    groups = active.reshape(active.shape[0], -1, local_blocks)
    most = jnp.broadcast_to(jnp.max(jnp.sum(groups, axis=(0, 2))), (8, 128))
    for shifts in (Y_SHIFT.values(), (HALF_SWAP,)):
        others = [lax.ppermute(most, "dp", shift) for shift in shifts]
        most = functools.reduce(jnp.maximum, others, most)
    return most[0, 0]


def make_slots(active, capacity):
    active = active.reshape(-1)
    pairs = jnp.arange(active.shape[0], dtype=jnp.int32)
    before = jnp.sum(jnp.where(pairs[None, :] < pairs[:, None], active[None, :], 0), axis=1)
    place = jnp.where(active > 0, before, -1)
    want = jnp.arange(capacity, dtype=jnp.int32)
    pair = jnp.sum(jnp.where(place[None, :] == want[:, None], pairs[None, :], 0), axis=1)
    return pair, jnp.sum(active)


def project_kernel(rhs_dims, blocks, pair_ref, core_ref, mine_ref, other_ref, w_ref, out_ref, x_ref, dense_ref):
    chips, rows = mine_ref.shape[0], mine_ref.shape[1]
    core = core_ref[0]
    for i in range(chips):
        for ref, at in ((mine_ref, 2 * i + core), (other_ref, 2 * i + 1 - core)):
            x_ref[pl.ds(pl.multiple_of(at * rows, rows), rows), :] = ref[i]
    wide = 2 * BLK
    for n in range(blocks // 2):
        cols = slice(n * wide, (n + 1) * wide)
        w = w_ref[:, cols] if rhs_dims == 0 else w_ref[cols, :]
        dense_ref[:, cols] = lax.dot_general(
            x_ref[...], w, (((1,), (rhs_dims,)), ((), ())), preferred_element_type=F32
        ).astype(BF16)

    def one(j, carry):
        pair = pair_ref[j]
        t = pl.multiple_of((pair // blocks) * BLK, BLK)
        f = pl.multiple_of((pair % blocks) * BLK, BLK)
        out_ref[pl.ds(pl.multiple_of(j * BLK, BLK), BLK), :] = dense_ref[pl.ds(t, BLK), pl.ds(f, BLK)]
        return carry

    lax.fori_loop(0, out_ref.shape[0] // BLK, one, 0)


def project(pair, core, mine, other, w, rhs_dims):
    depth = mine.shape[2]
    height = 2 * mine.shape[0] * mine.shape[1]
    width = w.shape[1 - rhs_dims]
    slots = pair.shape[0]
    return pl.pallas_call(
        functools.partial(project_kernel, rhs_dims, width // BLK),
        out_shape=(
            jax.ShapeDtypeStruct((slots * BLK, BLK), BF16),
            jax.ShapeDtypeStruct((height, depth), BF16),
        ),
        in_specs=[pl.BlockSpec(memory_space=pltpu.SMEM)] * 2
        + [pl.BlockSpec(memory_space=pltpu.VMEM)] * 3,
        out_specs=(pl.BlockSpec(memory_space=pltpu.VMEM), pl.BlockSpec(memory_space=pltpu.VMEM)),
        scratch_shapes=[pltpu.VMEM((height, width), BF16)],
        compiler_params=pltpu.CompilerParams(vmem_limit_bytes=24 << 20),
        cost_estimate=pl.CostEstimate(
            flops=2 * height * depth * width,
            bytes_accessed=2 * (height * depth + depth * width + slots * BLK * BLK),
            transcendentals=0,
        ),
    )(pair, core.reshape(1), mine, other, w)


def spread_kernel(blocks, share, pair_ref, info_ref, *refs):
    dense_ref = refs[-1]
    dense_ref[...] = jnp.zeros_like(dense_ref)
    place, count = info_ref[0], info_ref[1]
    piece = refs[0].shape[0] // BLK
    streams = share // piece
    for i, ref in enumerate(refs[:-1]):
        owner = place + i // streams + 1 - ROWS
        first = owner * share + (i % streams) * piece
        stop = jnp.where((owner >= 0) & (owner < ROWS), jnp.clip(count - first, 0, piece), 0)

        def one(j, carry, ref=ref, first=first):
            pair = pair_ref[first + j]
            t = pl.multiple_of((pair // blocks) * BLK, BLK)
            f = pl.multiple_of((pair % blocks) * BLK, BLK)
            dense_ref[pl.ds(t, BLK), pl.ds(f, BLK)] = ref[pl.ds(pl.multiple_of(j * BLK, BLK), BLK), :]
            return carry

        lax.fori_loop(0, stop, one, 0)


def spread(pair, info, pieces, height, width):
    return pl.pallas_call(
        functools.partial(spread_kernel, width // BLK, pair.shape[0] // ROWS),
        out_shape=jax.ShapeDtypeStruct((height, width), BF16),
        in_specs=[pl.BlockSpec(memory_space=pltpu.SMEM)] * 2
        + [pl.BlockSpec(memory_space=pltpu.VMEM)] * len(pieces),
        out_specs=pl.BlockSpec(memory_space=pltpu.VMEM),
        compiler_params=pltpu.CompilerParams(vmem_limit_bytes=24 << 20),
        cost_estimate=pl.CostEstimate(flops=0, bytes_accessed=8 * height * width, transcendentals=0),
    )(pair, info, *pieces)


def order_kernel(place_ref, *refs):
    for offset, ref in enumerate(refs[:-1]):
        refs[-1][(place_ref[0] + offset) % 4] = ref[...]


def gather_col(part, x, gate=lambda value: value):
    behind = lax.ppermute(part, "col", X_SHIFT[1])
    ahead = lax.ppermute(part, "col", X_SHIFT[3])
    far = lax.ppermute(part, "col", X_SHIFT[2])
    mine = pl.pallas_call(
        order_kernel,
        out_shape=jax.ShapeDtypeStruct((4, *part.shape), part.dtype),
        in_specs=[pl.BlockSpec(memory_space=pltpu.SMEM)] + [pl.BlockSpec(memory_space=pltpu.VMEM)] * 4,
        out_specs=pl.BlockSpec(memory_space=pltpu.VMEM),
        compiler_params=pltpu.CompilerParams(vmem_limit_bytes=8 << 20),
        cost_estimate=pl.CostEstimate(flops=0, bytes_accessed=16 * part.size, transcendentals=0),
    )(gate(x).reshape(1), part, ahead, far, behind)
    return mine, lax.ppermute(mine, "col", CORE_SWAP)


def scatter_row(compact, z):
    quarters = compact.reshape(ROWS, -1, BLK)
    sums = [pick(quarters, z)]
    for sign in (1, -1):
        got = None
        for step in range(1, ROWS):
            index = z + 4 - step if sign > 0 else z - 4 + step
            send = pick(quarters, jnp.clip(index, 0, ROWS - 1))
            if got is not None:
                send = add(send, got).astype(BF16)
            line = range(step) if sign > 0 else range(ROWS - 1, ROWS - 1 - step, -1)
            got = lax.ppermute(send, "row", [(i, i + sign) for i in line])
        sums.append(got)
    return add(*sums)


def gather_row(own, streams=1, gate=()):
    own = own.reshape(streams, -1, BLK)
    pieces = {(0, k): own[k] for k in range(streams)}
    for step in range(1, ROWS):
        for k in range(streams):
            for sign in (1, -1):
                line = range(step - 1, ROWS - 1) if sign > 0 else range(ROWS - step, 0, -1)
                send = pieces[-sign * (step - 1), k]
                if step == 2 and gate:
                    send = after(send, *gate)
                pieces[-sign * step, k] = lax.ppermute(send, "row", [(i, i + sign) for i in line])
    return [pieces[offset, k] for offset in range(1 - ROWS, ROWS) for k in range(streams)]


def scatter_ring(stack, i, axis, forward, backward):
    rows = stack.shape[1] // 2
    far = pick(stack, (i + 2) % 4)
    first = lax.ppermute(far[:rows], axis, forward)
    second = lax.ppermute(far[rows:], axis, backward)
    right = pick(stack, (i + 1) % 4)
    left = pick(stack, (i + 3) % 4)
    right = jnp.concatenate([add(right[:rows], first).astype(BF16), right[rows:]])
    left = jnp.concatenate([left[:rows], add(left[rows:], second).astype(BF16)])
    return add(
        pick(stack, i), lax.ppermute(right, axis, forward), lax.ppermute(left, axis, backward)
    )


def scatter_y(term, y):
    stack = term.reshape(4, term.shape[0] // 4, term.shape[1])
    return scatter_ring(stack, y, "dp", Y_SHIFT[1], Y_SHIFT[3])


def scatter_half(part, half, scale):
    halves = part.reshape(2, part.shape[0] // 2, part.shape[1])
    got = lax.ppermute(pick(halves, 1 - half).astype(BF16), "dp", HALF_SWAP)
    return (add(pick(halves, half), got) * scale).astype(BF16)


def scatter_col(term, x, core):
    stack = term.reshape(4, 2, term.shape[0] // 8, term.shape[1])
    keep = lax.dynamic_index_in_dim(stack, core, 1, keepdims=False)
    give = lax.dynamic_index_in_dim(stack, 1 - core, 1, keepdims=False)
    chip = add(keep, lax.ppermute(give, "col", CORE_SWAP)).astype(BF16)
    return scatter_ring(chip, x, "col", X_SHIFT[1], X_SHIFT[3]).astype(BF16)


def contract(lhs, rhs, left, right):
    return lax.dot_general(
        lhs, rhs, (((left,), (right,)), ((), ())), preferred_element_type=F32
    ).astype(BF16)


def run(capacity, parts, out_grad, in_weight, out_weight, active):
    dp, z, col = lax.axis_index("dp"), lax.axis_index("row"), lax.axis_index("col")
    y, half, x, core = dp // 2, dp % 2, col // 2, col % 2
    hidden_local = in_weight.shape[1]
    pair, count = make_slots(active, capacity)
    info = jnp.stack([z, count]).astype(jnp.int32)
    width = out_grad.shape[1] // 2

    pre, all_tokens = project(pair, core, *parts, in_weight, 0)
    height = all_tokens.shape[0]
    scale = (height * lax.axis_size("dp")) ** (-0.5)
    parts = gather_col(after(out_grad, pre), x)
    pre = scatter_row(pre, z)
    back, all_grad = project(pair, core, *parts, out_weight, 1)
    back = scatter_row(back, z)
    lifted = jax.nn.relu(pre)
    hidden = (lifted * lifted).astype(BF16)
    hidden_grad = (back * (2.0 * lifted)).astype(BF16)

    hidden = spread(pair, info, gather_row(hidden), height, hidden_local)
    out_term = contract(hidden, all_grad, 0, 0)
    pieces = gather_row(hidden_grad, 2 if capacity % (2 * ROWS) == 0 else 1, (out_term,))
    out_part = scatter_y(out_term, y)
    out_weight_grad = scatter_half(after(out_part, *pieces), half, scale)
    hidden_grad = spread(pair, info, pieces, height, hidden_local)
    in_weight_grad = jnp.concatenate(
        [
            scatter_half(scatter_y(contract(hidden_grad, cols, 0, 0), y), half, scale)
            for cols in (all_tokens[:, :width], all_tokens[:, width:])
        ],
        axis=1,
    )
    token_grad = scatter_col(contract(hidden_grad, in_weight, 1, 1), x, core)
    return (token_grad, in_weight_grad, out_weight_grad)


def body(tokens, out_grad, in_weight, out_weight, active_lists, active_counts):
    col = lax.axis_index("col")
    local_blocks = in_weight.shape[1] // BLK
    active = active_pairs(active_lists, active_counts, local_blocks * lax.axis_size("col"))
    most = most_pairs(active, local_blocks)
    active = lax.dynamic_slice_in_dim(active, col * local_blocks, local_blocks, 1)
    parts = gather_col(tokens, col // 2, lambda value: after(value, most))
    fits = sum((most > capacity).astype(jnp.int32) for capacity in CAPACITIES)
    branches = [
        functools.partial(run, capacity) for capacity in (*CAPACITIES, active.shape[0] * local_blocks)
    ]
    return lax.switch(fits, branches, parts, out_grad, in_weight, out_weight, active)


def solution(mesh):
    in_specs = (
        P(("dp", "col"), "row"),
        P(("dp", "col"), "row"),
        P("row", "col"),
        P("col", "row"),
        P("dp", None),
        P("dp"),
    )
    out_specs = (P(("dp", "col"), "row"), P(("col", "dp"), "row"), P(("col", "dp"), "row"))
    return jax.shard_map(body, mesh=mesh, in_specs=in_specs, out_specs=out_specs, check_vma=False)
```

```python
import functools

import jax
import jax.numpy as jnp
from jax import lax
from jax.experimental import pallas as pl
from jax.experimental.pallas import tpu as pltpu
from jax.sharding import PartitionSpec as P

BLK = 128
F32 = jnp.float32
BF16 = jnp.bfloat16
X_SHIFT = {s: [(c, ((c // 2 + s) % 4) * 2 + c % 2) for c in range(8)] for s in (1, 2, 3)}
CORE_SWAP = [(c, c ^ 1) for c in range(8)]
Y_SHIFT = {s: [(d, ((d // 2 + s) % 4) * 2 + d % 2) for d in range(8)] for s in (1, 2, 3)}
HALF_SWAP = [(d, d ^ 1) for d in range(8)]
ROWS = 4
CAPACITIES = (56,)


def pick(stack, index):
    return lax.dynamic_index_in_dim(stack, index, 0, keepdims=False)


def add(*terms):
    total = terms[0].astype(F32)
    for term in terms[1:]:
        total = total + term.astype(F32)
    return total


def after(value, *others):
    return lax.optimization_barrier((value, *others))[0]


def active_pairs(active_lists, active_counts, blocks):
    slots = jnp.arange(active_lists.shape[1], dtype=jnp.int32)
    valid = slots[None, :] < active_counts[:, None]
    wanted = jnp.arange(blocks, dtype=jnp.int32)
    hits = (active_lists[:, :, None] == wanted[None, None, :]) & valid[:, :, None]
    return jnp.any(hits, axis=1).astype(jnp.int32)


def most_pairs(active, local_blocks):
    groups = active.reshape(active.shape[0], -1, local_blocks)
    most = jnp.broadcast_to(jnp.max(jnp.sum(groups, axis=(0, 2))), (8, 128))
    for shifts in (Y_SHIFT.values(), (HALF_SWAP,)):
        others = [lax.ppermute(most, "dp", shift) for shift in shifts]
        most = functools.reduce(jnp.maximum, others, most)
    return most[0, 0]


def make_slots(active, capacity):
    active = active.reshape(-1)
    pairs = jnp.arange(active.shape[0], dtype=jnp.int32)
    before = jnp.sum(jnp.where(pairs[None, :] < pairs[:, None], active[None, :], 0), axis=1)
    place = jnp.where(active > 0, before, -1)
    want = jnp.arange(capacity, dtype=jnp.int32)
    pair = jnp.sum(jnp.where(place[None, :] == want[:, None], pairs[None, :], 0), axis=1)
    return pair, jnp.sum(active)


def project_kernel(rhs_dims, blocks, pair_ref, core_ref, mine_ref, other_ref, w_ref, out_ref, x_ref, dense_ref):
    chips, rows = mine_ref.shape[0], mine_ref.shape[1]
    core = core_ref[0]
    for i in range(chips):
        for ref, at in ((mine_ref, 2 * i + core), (other_ref, 2 * i + 1 - core)):
            x_ref[pl.ds(pl.multiple_of(at * rows, rows), rows), :] = ref[i]
    wide = 2 * BLK
    for n in range(blocks // 2):
        cols = slice(n * wide, (n + 1) * wide)
        w = w_ref[:, cols] if rhs_dims == 0 else w_ref[cols, :]
        dense_ref[:, cols] = lax.dot_general(
            x_ref[...], w, (((1,), (rhs_dims,)), ((), ())), preferred_element_type=F32
        ).astype(BF16)

    def one(j, carry):
        pair = pair_ref[j]
        t = pl.multiple_of((pair // blocks) * BLK, BLK)
        f = pl.multiple_of((pair % blocks) * BLK, BLK)
        out_ref[pl.ds(pl.multiple_of(j * BLK, BLK), BLK), :] = dense_ref[pl.ds(t, BLK), pl.ds(f, BLK)]
        return carry

    lax.fori_loop(0, out_ref.shape[0] // BLK, one, 0)


def project(pair, core, mine, other, w, rhs_dims):
    depth = mine.shape[2]
    height = 2 * mine.shape[0] * mine.shape[1]
    width = w.shape[1 - rhs_dims]
    slots = pair.shape[0]
    return pl.pallas_call(
        functools.partial(project_kernel, rhs_dims, width // BLK),
        out_shape=(
            jax.ShapeDtypeStruct((slots * BLK, BLK), BF16),
            jax.ShapeDtypeStruct((height, depth), BF16),
        ),
        in_specs=[pl.BlockSpec(memory_space=pltpu.SMEM)] * 2
        + [pl.BlockSpec(memory_space=pltpu.VMEM)] * 3,
        out_specs=(pl.BlockSpec(memory_space=pltpu.VMEM), pl.BlockSpec(memory_space=pltpu.VMEM)),
        scratch_shapes=[pltpu.VMEM((height, width), BF16)],
        compiler_params=pltpu.CompilerParams(vmem_limit_bytes=24 << 20),
        cost_estimate=pl.CostEstimate(
            flops=2 * height * depth * width,
            bytes_accessed=2 * (height * depth + depth * width + slots * BLK * BLK),
            transcendentals=0,
        ),
    )(pair, core.reshape(1), mine, other, w)


def spread_kernel(blocks, share, pair_ref, info_ref, *refs):
    dense_ref = refs[-1]
    dense_ref[...] = jnp.zeros_like(dense_ref)
    place, count = info_ref[0], info_ref[1]
    piece = refs[0].shape[0] // BLK
    streams = share // piece
    for i, ref in enumerate(refs[:-1]):
        owner = place + i // streams + 1 - ROWS
        first = owner * share + (i % streams) * piece
        stop = jnp.where((owner >= 0) & (owner < ROWS), jnp.clip(count - first, 0, piece), 0)

        def one(j, carry, ref=ref, first=first):
            pair = pair_ref[first + j]
            t = pl.multiple_of((pair // blocks) * BLK, BLK)
            f = pl.multiple_of((pair % blocks) * BLK, BLK)
            dense_ref[pl.ds(t, BLK), pl.ds(f, BLK)] = ref[pl.ds(pl.multiple_of(j * BLK, BLK), BLK), :]
            return carry

        lax.fori_loop(0, stop, one, 0)


def spread(pair, info, pieces, height, width):
    return pl.pallas_call(
        functools.partial(spread_kernel, width // BLK, pair.shape[0] // ROWS),
        out_shape=jax.ShapeDtypeStruct((height, width), BF16),
        in_specs=[pl.BlockSpec(memory_space=pltpu.SMEM)] * 2
        + [pl.BlockSpec(memory_space=pltpu.VMEM)] * len(pieces),
        out_specs=pl.BlockSpec(memory_space=pltpu.VMEM),
        compiler_params=pltpu.CompilerParams(vmem_limit_bytes=24 << 20),
        cost_estimate=pl.CostEstimate(flops=0, bytes_accessed=8 * height * width, transcendentals=0),
    )(pair, info, *pieces)


def order_kernel(place_ref, *refs):
    for offset, ref in enumerate(refs[:-1]):
        refs[-1][(place_ref[0] + offset) % 4] = ref[...]


def gather_col(part, x, gate=lambda value: value):
    behind = lax.ppermute(part, "col", X_SHIFT[1])
    ahead = lax.ppermute(part, "col", X_SHIFT[3])
    far = lax.ppermute(part, "col", X_SHIFT[2])
    mine = pl.pallas_call(
        order_kernel,
        out_shape=jax.ShapeDtypeStruct((4, *part.shape), part.dtype),
        in_specs=[pl.BlockSpec(memory_space=pltpu.SMEM)] + [pl.BlockSpec(memory_space=pltpu.VMEM)] * 4,
        out_specs=pl.BlockSpec(memory_space=pltpu.VMEM),
        compiler_params=pltpu.CompilerParams(vmem_limit_bytes=8 << 20),
        cost_estimate=pl.CostEstimate(flops=0, bytes_accessed=16 * part.size, transcendentals=0),
    )(gate(x).reshape(1), part, ahead, far, behind)
    return mine, lax.ppermute(mine, "col", CORE_SWAP)


def scatter_row(compact, z):
    quarters = compact.reshape(ROWS, -1, BLK)
    got = {}
    for step in range(1, ROWS):
        for sign in (1, -1):
            index = z + 4 - step if sign > 0 else z - 4 + step
            send = pick(quarters, jnp.clip(index, 0, ROWS - 1))
            if step > 1:
                send = add(send, got[sign, step - 1]).astype(BF16)
            line = range(step) if sign > 0 else range(ROWS - 1, ROWS - 1 - step, -1)
            got[sign, step] = lax.ppermute(send, "row", [(i, i + sign) for i in line])
    return add(pick(quarters, z), got[1, ROWS - 1], got[-1, ROWS - 1]), (got[1, 1], got[-1, 1])


def gather_row(own, gates={}):
    pieces = {0: own}
    for step in range(1, ROWS):
        for sign in (1, -1):
            line = range(step - 1, ROWS - 1) if sign > 0 else range(ROWS - step, 0, -1)
            send = after(pieces[-sign * (step - 1)], *gates.get(step, ()))
            pieces[-sign * step] = lax.ppermute(send, "row", [(i, i + sign) for i in line])
    return [pieces[offset] for offset in range(1 - ROWS, ROWS)]


def ring_first(stack, i, axis, forward, backward):
    rows = stack.shape[1] // 2
    far = pick(stack, (i + 2) % 4)
    return lax.ppermute(far[:rows], axis, forward), lax.ppermute(far[rows:], axis, backward)


def ring_second(stack, i, axis, forward, backward, first):
    rows = stack.shape[1] // 2
    right = pick(stack, (i + 1) % 4)
    left = pick(stack, (i + 3) % 4)
    right = jnp.concatenate([add(right[:rows], first[0]).astype(BF16), right[rows:]])
    left = jnp.concatenate([left[:rows], add(left[rows:], first[1]).astype(BF16)])
    return lax.ppermute(right, axis, forward), lax.ppermute(left, axis, backward)


def scatter_ring(stack, i, *ring):
    return add(pick(stack, i), *ring_second(stack, i, *ring, ring_first(stack, i, *ring)))


def y_parts(term):
    return term.reshape(4, term.shape[0] // 4, term.shape[1])


Y_RING = ("dp", Y_SHIFT[1], Y_SHIFT[3])


def scatter_half(part, half, scale):
    halves = part.reshape(2, part.shape[0] // 2, part.shape[1])
    got = lax.ppermute(pick(halves, 1 - half).astype(BF16), "dp", HALF_SWAP)
    return (add(pick(halves, half), got) * scale).astype(BF16)


def scatter_col(term, x, core):
    stack = term.reshape(4, 2, term.shape[0] // 8, term.shape[1])
    keep = lax.dynamic_index_in_dim(stack, core, 1, keepdims=False)
    give = lax.dynamic_index_in_dim(stack, 1 - core, 1, keepdims=False)
    chip = add(keep, lax.ppermute(give, "col", CORE_SWAP)).astype(BF16)
    return scatter_ring(chip, x, "col", X_SHIFT[1], X_SHIFT[3]).astype(BF16)


def contract(lhs, rhs, left, right):
    return lax.dot_general(
        lhs, rhs, (((left,), (right,)), ((), ())), preferred_element_type=F32
    ).astype(BF16)


def run(capacity, parts, out_grad, in_weight, out_weight, active):
    dp, z, col = lax.axis_index("dp"), lax.axis_index("row"), lax.axis_index("col")
    y, half, x, core = dp // 2, dp % 2, col // 2, col % 2
    hidden_local = in_weight.shape[1]
    pair, count = make_slots(active, capacity)
    info = jnp.stack([z, count]).astype(jnp.int32)
    width = out_grad.shape[1] // 2

    pre, all_tokens = project(pair, core, *parts, in_weight, 0)
    height = all_tokens.shape[0]
    scale = (height * lax.axis_size("dp")) ** (-0.5)
    out_grad = after(out_grad, pre)
    pre, first = scatter_row(pre, z)
    parts = gather_col(out_grad, x, lambda value: after(value, *first))
    lifted = jax.nn.relu(pre)
    pieces = gather_row((lifted * lifted).astype(BF16))
    back, all_grad = project(pair, core, *parts, out_weight, 1)
    back, _ = scatter_row(after(back, pieces[ROWS - 2], pieces[ROWS]), z)
    hidden_grad = (back * (2.0 * lifted)).astype(BF16)

    hidden = spread(pair, info, pieces, height, hidden_local)
    out_term = y_parts(contract(hidden, all_grad, 0, 0))
    first = ring_first(out_term, y, *Y_RING)
    pieces = gather_row(hidden_grad, {2: (out_term,), 3: first})
    second = ring_second(out_term, y, *Y_RING, first)
    pieces[0] = after(pieces[0], *second)
    hidden_grad = spread(pair, info, pieces, height, hidden_local)
    out_weight_grad = scatter_half(add(pick(out_term, y), *second), half, scale)
    in_weight_grad = jnp.concatenate(
        [
            scatter_half(scatter_ring(y_parts(contract(hidden_grad, cols, 0, 0)), y, *Y_RING), half, scale)
            for cols in (all_tokens[:, :width], all_tokens[:, width:])
        ],
        axis=1,
    )
    token_grad = scatter_col(contract(hidden_grad, in_weight, 1, 1), x, core)
    return (token_grad, in_weight_grad, out_weight_grad)


def body(tokens, out_grad, in_weight, out_weight, active_lists, active_counts):
    col = lax.axis_index("col")
    local_blocks = in_weight.shape[1] // BLK
    active = active_pairs(active_lists, active_counts, local_blocks * lax.axis_size("col"))
    most = most_pairs(active, local_blocks)
    active = lax.dynamic_slice_in_dim(active, col * local_blocks, local_blocks, 1)
    parts = gather_col(tokens, col // 2, lambda value: after(value, most))
    fits = sum((most > capacity).astype(jnp.int32) for capacity in CAPACITIES)
    branches = [
        functools.partial(run, capacity) for capacity in (*CAPACITIES, active.shape[0] * local_blocks)
    ]
    return lax.switch(fits, branches, parts, out_grad, in_weight, out_weight, active)


def solution(mesh):
    in_specs = (
        P(("dp", "col"), "row"),
        P(("dp", "col"), "row"),
        P("row", "col"),
        P("col", "row"),
        P("dp", None),
        P("dp"),
    )
    out_specs = (P(("dp", "col"), "row"), P(("col", "dp"), "row"), P(("col", "dp"), "row"))
    return jax.shard_map(body, mesh=mesh, in_specs=in_specs, out_specs=out_specs, check_vma=False)
```

```python
import functools

import jax
import jax.numpy as jnp
from jax import lax
from jax.experimental import pallas as pl
from jax.experimental.pallas import tpu as pltpu
from jax.sharding import PartitionSpec as P

BLK = 128
F32 = jnp.float32
BF16 = jnp.bfloat16
X_SHIFT = {s: [(c, ((c // 2 + s) % 4) * 2 + c % 2) for c in range(8)] for s in (1, 2, 3)}
CORE_SWAP = [(c, c ^ 1) for c in range(8)]
Y_SHIFT = {s: [(d, ((d // 2 + s) % 4) * 2 + d % 2) for d in range(8)] for s in (1, 2, 3)}
HALF_SWAP = [(d, d ^ 1) for d in range(8)]
ROWS = 4
CAPACITIES = (56,)


def pick(stack, index):
    return lax.dynamic_index_in_dim(stack, index, 0, keepdims=False)


def add(*terms):
    total = terms[0].astype(F32)
    for term in terms[1:]:
        total = total + term.astype(F32)
    return total


def after(value, *others):
    return lax.optimization_barrier((value, *others))[0]


def active_pairs(active_lists, active_counts, blocks):
    slots = jnp.arange(active_lists.shape[1], dtype=jnp.int32)
    valid = slots[None, :] < active_counts[:, None]
    wanted = jnp.arange(blocks, dtype=jnp.int32)
    hits = (active_lists[:, :, None] == wanted[None, None, :]) & valid[:, :, None]
    return jnp.any(hits, axis=1).astype(jnp.int32)


def most_pairs(active, local_blocks):
    groups = active.reshape(active.shape[0], -1, local_blocks)
    most = jnp.broadcast_to(jnp.max(jnp.sum(groups, axis=(0, 2))), (8, 128))
    for shifts in (Y_SHIFT.values(), (HALF_SWAP,)):
        others = [lax.ppermute(most, "dp", shift) for shift in shifts]
        most = functools.reduce(jnp.maximum, others, most)
    return most[0, 0]


def make_slots(active, capacity):
    active = active.reshape(-1)
    pairs = jnp.arange(active.shape[0], dtype=jnp.int32)
    before = jnp.sum(jnp.where(pairs[None, :] < pairs[:, None], active[None, :], 0), axis=1)
    place = jnp.where(active > 0, before, -1)
    want = jnp.arange(capacity, dtype=jnp.int32)
    pair = jnp.sum(jnp.where(place[None, :] == want[:, None], pairs[None, :], 0), axis=1)
    return pair, jnp.sum(active)


def project_kernel(rhs_dims, blocks, pair_ref, core_ref, mine_ref, other_ref, w_ref, out_ref, x_ref, dense_ref):
    chips, rows = mine_ref.shape[0], mine_ref.shape[1]
    core = core_ref[0]
    for i in range(chips):
        for ref, at in ((mine_ref, 2 * i + core), (other_ref, 2 * i + 1 - core)):
            x_ref[pl.ds(pl.multiple_of(at * rows, rows), rows), :] = ref[i]
    wide = 2 * BLK
    for n in range(blocks // 2):
        cols = slice(n * wide, (n + 1) * wide)
        w = w_ref[:, cols] if rhs_dims == 0 else w_ref[cols, :]
        dense_ref[:, cols] = lax.dot_general(
            x_ref[...], w, (((1,), (rhs_dims,)), ((), ())), preferred_element_type=F32
        ).astype(BF16)

    def one(j, carry):
        pair = pair_ref[j]
        t = pl.multiple_of((pair // blocks) * BLK, BLK)
        f = pl.multiple_of((pair % blocks) * BLK, BLK)
        out_ref[pl.ds(pl.multiple_of(j * BLK, BLK), BLK), :] = dense_ref[pl.ds(t, BLK), pl.ds(f, BLK)]
        return carry

    lax.fori_loop(0, out_ref.shape[0] // BLK, one, 0)


def project(pair, core, mine, other, w, rhs_dims):
    depth = mine.shape[2]
    height = 2 * mine.shape[0] * mine.shape[1]
    width = w.shape[1 - rhs_dims]
    slots = pair.shape[0]
    return pl.pallas_call(
        functools.partial(project_kernel, rhs_dims, width // BLK),
        out_shape=(
            jax.ShapeDtypeStruct((slots * BLK, BLK), BF16),
            jax.ShapeDtypeStruct((height, depth), BF16),
        ),
        in_specs=[pl.BlockSpec(memory_space=pltpu.SMEM)] * 2
        + [pl.BlockSpec(memory_space=pltpu.VMEM)] * 3,
        out_specs=(pl.BlockSpec(memory_space=pltpu.VMEM), pl.BlockSpec(memory_space=pltpu.VMEM)),
        scratch_shapes=[pltpu.VMEM((height, width), BF16)],
        compiler_params=pltpu.CompilerParams(vmem_limit_bytes=24 << 20),
        cost_estimate=pl.CostEstimate(
            flops=2 * height * depth * width,
            bytes_accessed=2 * (height * depth + depth * width + slots * BLK * BLK),
            transcendentals=0,
        ),
    )(pair, core.reshape(1), mine, other, w)


def spread_kernel(blocks, share, pair_ref, info_ref, *refs):
    dense_ref = refs[-1]
    dense_ref[...] = jnp.zeros_like(dense_ref)
    place, count = info_ref[0], info_ref[1]
    piece = refs[0].shape[0] // BLK
    streams = share // piece
    for i, ref in enumerate(refs[:-1]):
        owner = place + i // streams + 1 - ROWS
        first = owner * share + (i % streams) * piece
        stop = jnp.where((owner >= 0) & (owner < ROWS), jnp.clip(count - first, 0, piece), 0)

        def one(j, carry, ref=ref, first=first):
            pair = pair_ref[first + j]
            t = pl.multiple_of((pair // blocks) * BLK, BLK)
            f = pl.multiple_of((pair % blocks) * BLK, BLK)
            dense_ref[pl.ds(t, BLK), pl.ds(f, BLK)] = ref[pl.ds(pl.multiple_of(j * BLK, BLK), BLK), :]
            return carry

        lax.fori_loop(0, stop, one, 0)


def spread(pair, info, pieces, height, width):
    return pl.pallas_call(
        functools.partial(spread_kernel, width // BLK, pair.shape[0] // ROWS),
        out_shape=jax.ShapeDtypeStruct((height, width), BF16),
        in_specs=[pl.BlockSpec(memory_space=pltpu.SMEM)] * 2
        + [pl.BlockSpec(memory_space=pltpu.VMEM)] * len(pieces),
        out_specs=pl.BlockSpec(memory_space=pltpu.VMEM),
        compiler_params=pltpu.CompilerParams(vmem_limit_bytes=24 << 20),
        cost_estimate=pl.CostEstimate(flops=0, bytes_accessed=8 * height * width, transcendentals=0),
    )(pair, info, *pieces)


def order_kernel(place_ref, *refs):
    for offset, ref in enumerate(refs[:-1]):
        refs[-1][(place_ref[0] + offset) % 4] = ref[...]


def gather_col(part, x, gate=lambda value: value):
    behind = lax.ppermute(part, "col", X_SHIFT[1])
    ahead = lax.ppermute(part, "col", X_SHIFT[3])
    far = lax.ppermute(part, "col", X_SHIFT[2])
    mine = pl.pallas_call(
        order_kernel,
        out_shape=jax.ShapeDtypeStruct((4, *part.shape), part.dtype),
        in_specs=[pl.BlockSpec(memory_space=pltpu.SMEM)] + [pl.BlockSpec(memory_space=pltpu.VMEM)] * 4,
        out_specs=pl.BlockSpec(memory_space=pltpu.VMEM),
        compiler_params=pltpu.CompilerParams(vmem_limit_bytes=8 << 20),
        cost_estimate=pl.CostEstimate(flops=0, bytes_accessed=16 * part.size, transcendentals=0),
    )(gate(x).reshape(1), part, ahead, far, behind)
    return mine, lax.ppermute(mine, "col", CORE_SWAP)


def scatter_row(compact, z, gates={}):
    quarters = compact.reshape(ROWS, -1, BLK)
    got = {}
    for step in range(1, ROWS):
        for sign in (1, -1):
            index = z + 4 - step if sign > 0 else z - 4 + step
            send = pick(quarters, jnp.clip(index, 0, ROWS - 1))
            if step > 1:
                send = add(send, got[sign, step - 1]).astype(BF16)
            send = after(send, *gates.get(step, ()))
            line = range(step) if sign > 0 else range(ROWS - 1, ROWS - 1 - step, -1)
            got[sign, step] = lax.ppermute(send, "row", [(i, i + sign) for i in line])
    return add(pick(quarters, z), got[1, ROWS - 1], got[-1, ROWS - 1])


def gather_row(own, gates={}):
    pieces = {0: own}
    for step in range(1, ROWS):
        for sign in (1, -1):
            line = range(step - 1, ROWS - 1) if sign > 0 else range(ROWS - step, 0, -1)
            send = after(pieces[-sign * (step - 1)], *gates.get(step, ()))
            pieces[-sign * step] = lax.ppermute(send, "row", [(i, i + sign) for i in line])
    return [pieces[offset] for offset in range(1 - ROWS, ROWS)]


def ring_first(stack, i, axis, forward, backward):
    rows = stack.shape[1] // 2
    far = pick(stack, (i + 2) % 4)
    return lax.ppermute(far[:rows], axis, forward), lax.ppermute(far[rows:], axis, backward)


def ring_second(stack, i, axis, forward, backward, first):
    rows = stack.shape[1] // 2
    right = pick(stack, (i + 1) % 4)
    left = pick(stack, (i + 3) % 4)
    right = jnp.concatenate([add(right[:rows], first[0]).astype(BF16), right[rows:]])
    left = jnp.concatenate([left[:rows], add(left[rows:], first[1]).astype(BF16)])
    return lax.ppermute(right, axis, forward), lax.ppermute(left, axis, backward)


def scatter_ring(stack, i, *ring):
    return add(pick(stack, i), *ring_second(stack, i, *ring, ring_first(stack, i, *ring)))


def y_parts(term):
    return term.reshape(4, term.shape[0] // 4, term.shape[1])


Y_RING = ("dp", Y_SHIFT[1], Y_SHIFT[3])


def scatter_half(part, half, scale):
    halves = part.reshape(2, part.shape[0] // 2, part.shape[1])
    got = lax.ppermute(pick(halves, 1 - half).astype(BF16), "dp", HALF_SWAP)
    return (add(pick(halves, half), got) * scale).astype(BF16)


def scatter_col(term, x, core):
    stack = term.reshape(4, 2, term.shape[0] // 8, term.shape[1])
    keep = lax.dynamic_index_in_dim(stack, core, 1, keepdims=False)
    give = lax.dynamic_index_in_dim(stack, 1 - core, 1, keepdims=False)
    chip = add(keep, lax.ppermute(give, "col", CORE_SWAP)).astype(BF16)
    return scatter_ring(chip, x, "col", X_SHIFT[1], X_SHIFT[3]).astype(BF16)


def contract(lhs, rhs, left, right):
    return lax.dot_general(
        lhs, rhs, (((left,), (right,)), ((), ())), preferred_element_type=F32
    ).astype(BF16)


def run(capacity, token_parts, grad_parts, in_weight, out_weight, active):
    dp, z, col = lax.axis_index("dp"), lax.axis_index("row"), lax.axis_index("col")
    y, half, x, core = dp // 2, dp % 2, col // 2, col % 2
    hidden_local = in_weight.shape[1]
    pair, count = make_slots(active, capacity)
    info = jnp.stack([z, count]).astype(jnp.int32)
    pre, all_tokens = project(pair, core, *token_parts, in_weight, 0)
    height, width = all_tokens.shape[0], all_tokens.shape[1] // 2
    scale = (height * lax.axis_size("dp")) ** (-0.5)
    back, all_grad = project(pair, core, *grad_parts, out_weight, 1)
    pre = scatter_row(pre, z, {2: (back,)})
    lifted = jax.nn.relu(pre)
    pieces = gather_row((lifted * lifted).astype(BF16))
    back = scatter_row(after(back, pieces[ROWS - 2], pieces[ROWS]), z)
    hidden_grad = (back * (2.0 * lifted)).astype(BF16)

    hidden = spread(pair, info, pieces, height, hidden_local)
    out_term = y_parts(contract(hidden, all_grad, 0, 0))
    first = ring_first(out_term, y, *Y_RING)
    pieces = gather_row(hidden_grad, {2: (out_term,), 3: first})
    second = ring_second(out_term, y, *Y_RING, first)
    pieces[0] = after(pieces[0], *second)
    hidden_grad = spread(pair, info, pieces, height, hidden_local)
    in_terms = [
        y_parts(contract(hidden_grad, cols, 0, 0))
        for cols in (all_tokens[:, :width], all_tokens[:, width:])
    ]
    out_part = after(add(pick(out_term, y), *second), *in_terms)
    out_weight_grad = scatter_half(out_part, half, scale)
    in_weight_grad = jnp.concatenate(
        [scatter_half(scatter_ring(term, y, *Y_RING), half, scale) for term in in_terms], axis=1
    )
    token_grad = scatter_col(contract(hidden_grad, in_weight, 1, 1), x, core)
    return (token_grad, in_weight_grad, out_weight_grad)


def body(tokens, out_grad, in_weight, out_weight, active_lists, active_counts):
    col = lax.axis_index("col")
    local_blocks = in_weight.shape[1] // BLK
    active = active_pairs(active_lists, active_counts, local_blocks * lax.axis_size("col"))
    most = most_pairs(active, local_blocks)
    active = lax.dynamic_slice_in_dim(active, col * local_blocks, local_blocks, 1)
    token_parts = gather_col(tokens, col // 2, lambda value: after(value, most))
    grad_parts = gather_col(out_grad, col // 2, lambda value: after(value, most))
    fits = sum((most > capacity).astype(jnp.int32) for capacity in CAPACITIES)
    branches = [
        functools.partial(run, capacity) for capacity in (*CAPACITIES, active.shape[0] * local_blocks)
    ]
    return lax.switch(fits, branches, token_parts, grad_parts, in_weight, out_weight, active)


def solution(mesh):
    in_specs = (
        P(("dp", "col"), "row"),
        P(("dp", "col"), "row"),
        P("row", "col"),
        P("col", "row"),
        P("dp", None),
        P("dp"),
    )
    out_specs = (P(("dp", "col"), "row"), P(("col", "dp"), "row"), P(("col", "dp"), "row"))
    return jax.shard_map(body, mesh=mesh, in_specs=in_specs, out_specs=out_specs, check_vma=False)
```

```python
import functools

import jax
import jax.numpy as jnp
from jax import lax
from jax.experimental import pallas as pl
from jax.experimental.pallas import tpu as pltpu
from jax.sharding import PartitionSpec as P

BLK = 128
F32 = jnp.float32
BF16 = jnp.bfloat16
X_SHIFT = {s: [(c, ((c // 2 + s) % 4) * 2 + c % 2) for c in range(8)] for s in (1, 2, 3)}
CORE_SWAP = [(c, c ^ 1) for c in range(8)]
Y_SHIFT = {s: [(d, ((d // 2 + s) % 4) * 2 + d % 2) for d in range(8)] for s in (1, 2, 3)}
HALF_SWAP = [(d, d ^ 1) for d in range(8)]
ROWS = 4
CAPACITIES = (56,)


def pick(stack, index):
    return lax.dynamic_index_in_dim(stack, index, 0, keepdims=False)


def add(*terms):
    total = terms[0].astype(F32)
    for term in terms[1:]:
        total = total + term.astype(F32)
    return total


def after(value, *others):
    return lax.optimization_barrier((value, *others))[0]


def active_pairs(active_lists, active_counts, blocks):
    slots = jnp.arange(active_lists.shape[1], dtype=jnp.int32)
    valid = slots[None, :] < active_counts[:, None]
    wanted = jnp.arange(blocks, dtype=jnp.int32)
    hits = (active_lists[:, :, None] == wanted[None, None, :]) & valid[:, :, None]
    return jnp.any(hits, axis=1).astype(jnp.int32)


def most_pairs(active, local_blocks):
    groups = active.reshape(active.shape[0], -1, local_blocks)
    most = jnp.broadcast_to(jnp.max(jnp.sum(groups, axis=(0, 2))), (8, 128))
    for shift in (Y_SHIFT[1], Y_SHIFT[2]):
        most = jnp.maximum(most, lax.ppermute(most, "dp", shift))
    return most


def make_slots(active, capacity):
    active = active.reshape(-1)
    pairs = jnp.arange(active.shape[0], dtype=jnp.int32)
    before = jnp.sum(jnp.where(pairs[None, :] < pairs[:, None], active[None, :], 0), axis=1)
    place = jnp.where(active > 0, before, -1)
    want = jnp.arange(capacity, dtype=jnp.int32)
    pair = jnp.sum(jnp.where(place[None, :] == want[:, None], pairs[None, :], 0), axis=1)
    return pair, jnp.sum(active)


def project_kernel(rhs_dims, blocks, pair_ref, core_ref, mine_ref, other_ref, w_ref, out_ref, x_ref, dense_ref):
    chips, rows = mine_ref.shape[0], mine_ref.shape[1]
    core = core_ref[0]
    for i in range(chips):
        for ref, at in ((mine_ref, 2 * i + core), (other_ref, 2 * i + 1 - core)):
            x_ref[pl.ds(pl.multiple_of(at * rows, rows), rows), :] = ref[i]
    wide = 2 * BLK
    for n in range(blocks // 2):
        cols = slice(n * wide, (n + 1) * wide)
        w = w_ref[:, cols] if rhs_dims == 0 else w_ref[cols, :]
        dense_ref[:, cols] = lax.dot_general(
            x_ref[...], w, (((1,), (rhs_dims,)), ((), ())), preferred_element_type=F32
        ).astype(BF16)

    def one(j, carry):
        pair = pair_ref[j]
        t = pl.multiple_of((pair // blocks) * BLK, BLK)
        f = pl.multiple_of((pair % blocks) * BLK, BLK)
        out_ref[pl.ds(pl.multiple_of(j * BLK, BLK), BLK), :] = dense_ref[pl.ds(t, BLK), pl.ds(f, BLK)]
        return carry

    lax.fori_loop(0, out_ref.shape[0] // BLK, one, 0)


def project(pair, core, mine, other, w, rhs_dims):
    depth = mine.shape[2]
    height = 2 * mine.shape[0] * mine.shape[1]
    width = w.shape[1 - rhs_dims]
    slots = pair.shape[0]
    return pl.pallas_call(
        functools.partial(project_kernel, rhs_dims, width // BLK),
        out_shape=(
            jax.ShapeDtypeStruct((slots * BLK, BLK), BF16),
            jax.ShapeDtypeStruct((height, depth), BF16),
        ),
        in_specs=[pl.BlockSpec(memory_space=pltpu.SMEM)] * 2
        + [pl.BlockSpec(memory_space=pltpu.VMEM)] * 3,
        out_specs=(pl.BlockSpec(memory_space=pltpu.VMEM), pl.BlockSpec(memory_space=pltpu.VMEM)),
        scratch_shapes=[pltpu.VMEM((height, width), BF16)],
        compiler_params=pltpu.CompilerParams(vmem_limit_bytes=24 << 20),
        cost_estimate=pl.CostEstimate(
            flops=2 * height * depth * width,
            bytes_accessed=2 * (height * depth + depth * width + slots * BLK * BLK),
            transcendentals=0,
        ),
    )(pair, core.reshape(1), mine, other, w)


def spread_kernel(blocks, share, pair_ref, info_ref, *refs):
    dense_ref = refs[-1]
    dense_ref[...] = jnp.zeros_like(dense_ref)
    place, count = info_ref[0], info_ref[1]
    piece = refs[0].shape[0] // BLK
    streams = share // piece
    for i, ref in enumerate(refs[:-1]):
        owner = place + i // streams + 1 - ROWS
        first = owner * share + (i % streams) * piece
        stop = jnp.where((owner >= 0) & (owner < ROWS), jnp.clip(count - first, 0, piece), 0)

        def one(j, carry, ref=ref, first=first):
            pair = pair_ref[first + j]
            t = pl.multiple_of((pair // blocks) * BLK, BLK)
            f = pl.multiple_of((pair % blocks) * BLK, BLK)
            dense_ref[pl.ds(t, BLK), pl.ds(f, BLK)] = ref[pl.ds(pl.multiple_of(j * BLK, BLK), BLK), :]
            return carry

        lax.fori_loop(0, stop, one, 0)


def spread(pair, info, pieces, height, width):
    return pl.pallas_call(
        functools.partial(spread_kernel, width // BLK, pair.shape[0] // ROWS),
        out_shape=jax.ShapeDtypeStruct((height, width), BF16),
        in_specs=[pl.BlockSpec(memory_space=pltpu.SMEM)] * 2
        + [pl.BlockSpec(memory_space=pltpu.VMEM)] * len(pieces),
        out_specs=pl.BlockSpec(memory_space=pltpu.VMEM),
        compiler_params=pltpu.CompilerParams(vmem_limit_bytes=24 << 20),
        cost_estimate=pl.CostEstimate(flops=0, bytes_accessed=8 * height * width, transcendentals=0),
    )(pair, info, *pieces)


def order_kernel(place_ref, *refs):
    for offset, ref in enumerate(refs[:-1]):
        refs[-1][(place_ref[0] + offset) % 4] = ref[...]


def gather_x(part):
    behind = lax.ppermute(part, "col", X_SHIFT[1])
    ahead = lax.ppermute(part, "col", X_SHIFT[3])
    far = lax.ppermute(part, "col", X_SHIFT[2])
    return part, ahead, far, behind


def gather_core(ring, x):
    part = ring[0]
    mine = pl.pallas_call(
        order_kernel,
        out_shape=jax.ShapeDtypeStruct((4, *part.shape), part.dtype),
        in_specs=[pl.BlockSpec(memory_space=pltpu.SMEM)] + [pl.BlockSpec(memory_space=pltpu.VMEM)] * 4,
        out_specs=pl.BlockSpec(memory_space=pltpu.VMEM),
        compiler_params=pltpu.CompilerParams(vmem_limit_bytes=8 << 20),
        cost_estimate=pl.CostEstimate(flops=0, bytes_accessed=16 * part.size, transcendentals=0),
    )(x.reshape(1), *ring)
    return mine, lax.ppermute(mine, "col", CORE_SWAP)


def together(*values):
    return lax.optimization_barrier(values)


LINE = {
    sign: {step: [(i, i + sign) for i in line[:step]] for step in range(1, ROWS)}
    for sign, line in ((1, range(ROWS - 1)), (-1, range(ROWS - 1, 0, -1)))
}
ENDS_IN = LINE[1][1] + LINE[-1][1]
ENDS_OUT = [(2, 3), (1, 0)]


def scatter_row(compact, z, gates={}):
    quarters = compact.reshape(ROWS, -1, BLK)

    def own(index):
        return pick(quarters, jnp.clip(index, 0, ROWS - 1))

    def sender(got, index, here):
        return jnp.where(here, add(own(index), got), own(index).astype(F32)).astype(BF16)

    got = lax.ppermute(own(ROWS - 1 - z), "row", ENDS_IN)
    up, down = together(
        sender(got, z + 2, z == 1), sender(got, z - 2, z == 2), *gates.get(2, ())
    )[:2]
    up = lax.ppermute(up, "row", LINE[1][2])
    down = lax.ppermute(down, "row", LINE[-1][2])
    up, down = together(
        add(own(z + 1), up).astype(BF16), add(own(z - 1), down).astype(BF16), *gates.get(3, ())
    )[:2]
    up = lax.ppermute(up, "row", LINE[1][3])
    down = lax.ppermute(down, "row", LINE[-1][3])
    return add(own(z), up, down)


def gather_row(own, z, gates={}):
    below = lax.ppermute(own, "row", LINE[1][3])
    above = lax.ppermute(own, "row", LINE[-1][3])
    up, down = together(below, above, *gates.get(2, ()))[:2]
    below2 = lax.ppermute(up, "row", LINE[1][3][1:])
    above2 = lax.ppermute(down, "row", LINE[-1][3][1:])
    last = after(jnp.where(z == 2, below2, above2), *gates.get(3, ()))
    last = lax.ppermute(last, "row", ENDS_OUT)
    return [last, below2, below, own, above, above2, last]


def ring_first(stack, i, axis, forward, backward):
    rows = stack.shape[1] // 2
    far = pick(stack, (i + 2) % 4)
    return lax.ppermute(far[:rows], axis, forward), lax.ppermute(far[rows:], axis, backward)


def ring_second(stack, i, axis, forward, backward, first):
    rows = stack.shape[1] // 2
    right = pick(stack, (i + 1) % 4)
    left = pick(stack, (i + 3) % 4)
    right = jnp.concatenate([add(right[:rows], first[0]).astype(BF16), right[rows:]])
    left = jnp.concatenate([left[:rows], add(left[rows:], first[1]).astype(BF16)])
    return lax.ppermute(right, axis, forward), lax.ppermute(left, axis, backward)


def scatter_ring(stack, i, *ring):
    return add(pick(stack, i), *ring_second(stack, i, *ring, ring_first(stack, i, *ring)))


def y_parts(term):
    return term.reshape(4, term.shape[0] // 4, term.shape[1])


Y_RING = ("dp", Y_SHIFT[1], Y_SHIFT[3])


def scatter_half(part, half, scale):
    halves = part.reshape(2, part.shape[0] // 2, part.shape[1])
    got = lax.ppermute(pick(halves, 1 - half).astype(BF16), "dp", HALF_SWAP)
    return (add(pick(halves, half), got) * scale).astype(BF16)


def scatter_col(term, x, core):
    stack = term.reshape(4, 2, term.shape[0] // 8, term.shape[1])
    keep = lax.dynamic_index_in_dim(stack, core, 1, keepdims=False)
    give = lax.dynamic_index_in_dim(stack, 1 - core, 1, keepdims=False)
    chip = add(keep, lax.ppermute(give, "col", CORE_SWAP)).astype(BF16)
    return scatter_ring(chip, x, "col", X_SHIFT[1], X_SHIFT[3]).astype(BF16)


def contract(lhs, rhs, left, right):
    return lax.dot_general(
        lhs, rhs, (((left,), (right,)), ((), ())), preferred_element_type=F32
    ).astype(BF16)


def run(capacity, token_parts, grad_parts, in_weight, out_weight, active):
    dp, z, col = lax.axis_index("dp"), lax.axis_index("row"), lax.axis_index("col")
    y, half, x, core = dp // 2, dp % 2, col // 2, col % 2
    hidden_local = in_weight.shape[1]
    pair, count = make_slots(active, capacity)
    info = jnp.stack([z, count]).astype(jnp.int32)
    pre, all_tokens = project(pair, core, *token_parts, in_weight, 0)
    height, width = all_tokens.shape[0], all_tokens.shape[1] // 2
    scale = (height * lax.axis_size("dp")) ** (-0.5)
    back, all_grad = project(pair, core, *grad_parts, out_weight, 1)
    pre = scatter_row(pre, z, {2: (back,)})
    lifted = jax.nn.relu(pre)
    pieces = gather_row((lifted * lifted).astype(BF16), z)
    back = scatter_row(after(back, pieces[ROWS - 2], pieces[ROWS]), z)
    hidden_grad = (back * (2.0 * lifted)).astype(BF16)

    hidden = spread(pair, info, pieces, height, hidden_local)
    out_term = y_parts(contract(hidden, all_grad, 0, 0))
    first = ring_first(out_term, y, *Y_RING)
    pieces = gather_row(hidden_grad, z, {2: (out_term,), 3: first})
    second = ring_second(out_term, y, *Y_RING, first)
    pieces[0] = after(pieces[0], *second)
    hidden_grad = spread(pair, info, pieces, height, hidden_local)
    in_terms = [
        y_parts(contract(hidden_grad, cols, 0, 0))
        for cols in (all_tokens[:, :width], all_tokens[:, width:])
    ]
    out_part = after(add(pick(out_term, y), *second), *in_terms)
    out_weight_grad = scatter_half(out_part, half, scale)
    in_weight_grad = jnp.concatenate(
        [scatter_half(scatter_ring(term, y, *Y_RING), half, scale) for term in in_terms], axis=1
    )
    token_grad = scatter_col(contract(hidden_grad, in_weight, 1, 1), x, core)
    return (token_grad, in_weight_grad, out_weight_grad)


def body(tokens, out_grad, in_weight, out_weight, active_lists, active_counts):
    col = lax.axis_index("col")
    local_blocks = in_weight.shape[1] // BLK
    active = active_pairs(active_lists, active_counts, local_blocks * lax.axis_size("col"))
    most = most_pairs(active, local_blocks)
    active = lax.dynamic_slice_in_dim(active, col * local_blocks, local_blocks, 1)
    ring = gather_x(tokens)
    most, out_grad = together(most, out_grad, *ring[1:])[:2]
    grad_ring = gather_x(out_grad)
    most = jnp.maximum(most, lax.ppermute(most, "dp", HALF_SWAP))
    token_parts = gather_core(ring, col // 2)
    grad_parts = gather_core((after(grad_ring[0], most), *grad_ring[1:]), col // 2)
    most = most[0, 0]
    fits = sum((most > capacity).astype(jnp.int32) for capacity in CAPACITIES)
    branches = [
        functools.partial(run, capacity) for capacity in (*CAPACITIES, active.shape[0] * local_blocks)
    ]
    return lax.switch(fits, branches, token_parts, grad_parts, in_weight, out_weight, active)


def solution(mesh):
    in_specs = (
        P(("dp", "col"), "row"),
        P(("dp", "col"), "row"),
        P("row", "col"),
        P("col", "row"),
        P("dp", None),
        P("dp"),
    )
    out_specs = (P(("dp", "col"), "row"), P(("col", "dp"), "row"), P(("col", "dp"), "row"))
    return jax.shard_map(body, mesh=mesh, in_specs=in_specs, out_specs=out_specs, check_vma=False)
```

```python
import functools

import jax
import jax.numpy as jnp
from jax import lax
from jax.experimental import pallas as pl
from jax.experimental.pallas import tpu as pltpu
from jax.sharding import PartitionSpec as P

BLK = 128
F32 = jnp.float32
BF16 = jnp.bfloat16
X_SHIFT = {s: [(c, ((c // 2 + s) % 4) * 2 + c % 2) for c in range(8)] for s in (1, 2, 3)}
CORE_SWAP = [(c, c ^ 1) for c in range(8)]
Y_SHIFT = {s: [(d, ((d // 2 + s) % 4) * 2 + d % 2) for d in range(8)] for s in (1, 2, 3)}
HALF_SWAP = [(d, d ^ 1) for d in range(8)]
ROWS = 4
CAPACITIES = (56,)


def pick(stack, index):
    return lax.dynamic_index_in_dim(stack, index, 0, keepdims=False)


def add(*terms):
    total = terms[0].astype(F32)
    for term in terms[1:]:
        total = total + term.astype(F32)
    return total


def after(value, *others):
    return lax.optimization_barrier((value, *others))[0]


def active_pairs(active_lists, active_counts, blocks):
    slots = jnp.arange(active_lists.shape[1], dtype=jnp.int32)
    valid = slots[None, :] < active_counts[:, None]
    wanted = jnp.arange(blocks, dtype=jnp.int32)
    hits = (active_lists[:, :, None] == wanted[None, None, :]) & valid[:, :, None]
    return jnp.any(hits, axis=1).astype(jnp.int32)


def most_pairs(active, local_blocks):
    groups = active.reshape(active.shape[0], -1, local_blocks)
    most = jnp.broadcast_to(jnp.max(jnp.sum(groups, axis=(0, 2))), (8, 128))
    for shift in (Y_SHIFT[1], Y_SHIFT[2]):
        most = jnp.maximum(most, lax.ppermute(most, "dp", shift))
    return most


def make_slots(active, capacity):
    active = active.reshape(-1)
    pairs = jnp.arange(active.shape[0], dtype=jnp.int32)
    before = jnp.sum(jnp.where(pairs[None, :] < pairs[:, None], active[None, :], 0), axis=1)
    place = jnp.where(active > 0, before, -1)
    want = jnp.arange(capacity, dtype=jnp.int32)
    pair = jnp.sum(jnp.where(place[None, :] == want[:, None], pairs[None, :], 0), axis=1)
    return pair, jnp.sum(active)


def join(core, mine_ref, other_ref, x_ref):
    chips, rows = mine_ref.shape[0], mine_ref.shape[1]
    for i in range(chips):
        for ref, at in ((mine_ref, 2 * i + core), (other_ref, 2 * i + 1 - core)):
            x_ref[pl.ds(pl.multiple_of(at * rows, rows), rows), :] = ref[i]


def multiply(rhs_dims, x_ref, w_ref, dense_ref):
    wide = 2 * BLK

    def one(n, carry):
        cols = pl.ds(pl.multiple_of(n * wide, wide), wide)
        w = w_ref[:, cols] if rhs_dims == 0 else w_ref[cols, :]
        dense_ref[:, cols] = lax.dot_general(
            x_ref[...], w, (((1,), (rhs_dims,)), ((), ())), preferred_element_type=F32
        ).astype(BF16)
        return carry

    lax.fori_loop(0, dense_ref.shape[1] // wide, one, 0)


def compact_kernel(pair_ref, dense_ref, out_ref):
    blocks = dense_ref.shape[1] // BLK

    def one(j, carry):
        pair = pair_ref[j]
        t = pl.multiple_of((pair // blocks) * BLK, BLK)
        f = pl.multiple_of((pair % blocks) * BLK, BLK)
        out_ref[pl.ds(pl.multiple_of(j * BLK, BLK), BLK), :] = dense_ref[pl.ds(t, BLK), pl.ds(f, BLK)]
        return carry

    lax.fori_loop(0, out_ref.shape[0] // BLK, one, 0)


def dense_kernel(rhs_dims, core_ref, mine_ref, other_ref, w_ref, x_ref, dense_ref):
    join(core_ref[0], mine_ref, other_ref, x_ref)
    multiply(rhs_dims, x_ref, w_ref, dense_ref)


def project_kernel(rhs_dims, pair_ref, core_ref, mine_ref, other_ref, w_ref, x_ref, out_ref, dense_ref):
    join(core_ref[0], mine_ref, other_ref, x_ref)
    multiply(rhs_dims, x_ref, w_ref, dense_ref)
    compact_kernel(pair_ref, dense_ref, out_ref)


def compact(pair, dense):
    shape = (pair.shape[0] * BLK, BLK)
    return pl.pallas_call(
        compact_kernel,
        out_shape=jax.ShapeDtypeStruct(shape, BF16),
        in_specs=[pl.BlockSpec(memory_space=pltpu.SMEM), pl.BlockSpec(memory_space=pltpu.VMEM)],
        out_specs=pl.BlockSpec(memory_space=pltpu.VMEM),
        compiler_params=pltpu.CompilerParams(vmem_limit_bytes=16 << 20),
        cost_estimate=pl.CostEstimate(
            flops=0, bytes_accessed=2 * (dense.size + shape[0] * BLK), transcendentals=0
        ),
    )(pair, dense)


def project(core, mine, other, w, rhs_dims, pair=None):
    depth = mine.shape[2]
    height = 2 * mine.shape[0] * mine.shape[1]
    width = w.shape[1 - rhs_dims]
    dense = (height, width)
    result = dense if pair is None else (pair.shape[0] * BLK, BLK)
    scalars = [core.reshape(1)] if pair is None else [pair, core.reshape(1)]
    return pl.pallas_call(
        functools.partial(dense_kernel if pair is None else project_kernel, rhs_dims),
        out_shape=(jax.ShapeDtypeStruct((height, depth), BF16), jax.ShapeDtypeStruct(result, BF16)),
        in_specs=[pl.BlockSpec(memory_space=pltpu.SMEM)] * len(scalars)
        + [pl.BlockSpec(memory_space=pltpu.VMEM)] * 3,
        out_specs=(pl.BlockSpec(memory_space=pltpu.VMEM), pl.BlockSpec(memory_space=pltpu.VMEM)),
        scratch_shapes=[] if pair is None else [pltpu.VMEM(dense, BF16)],
        compiler_params=pltpu.CompilerParams(vmem_limit_bytes=24 << 20),
        cost_estimate=pl.CostEstimate(
            flops=2 * height * depth * width,
            bytes_accessed=2 * (height * depth + depth * width + result[0] * result[1]),
            transcendentals=0,
        ),
    )(*scalars, mine, other, w)


def spread_kernel(blocks, share, pair_ref, info_ref, *refs):
    dense_ref = refs[-1]
    dense_ref[...] = jnp.zeros_like(dense_ref)
    place, count = info_ref[0], info_ref[1]
    piece = refs[0].shape[0] // BLK
    streams = share // piece
    for i, ref in enumerate(refs[:-1]):
        owner = place + i // streams + 1 - ROWS
        first = owner * share + (i % streams) * piece
        stop = jnp.where((owner >= 0) & (owner < ROWS), jnp.clip(count - first, 0, piece), 0)

        def one(j, carry, ref=ref, first=first):
            pair = pair_ref[first + j]
            t = pl.multiple_of((pair // blocks) * BLK, BLK)
            f = pl.multiple_of((pair % blocks) * BLK, BLK)
            dense_ref[pl.ds(t, BLK), pl.ds(f, BLK)] = ref[pl.ds(pl.multiple_of(j * BLK, BLK), BLK), :]
            return carry

        lax.fori_loop(0, stop, one, 0)


def spread(pair, info, pieces, height, width):
    return pl.pallas_call(
        functools.partial(spread_kernel, width // BLK, pair.shape[0] // ROWS),
        out_shape=jax.ShapeDtypeStruct((height, width), BF16),
        in_specs=[pl.BlockSpec(memory_space=pltpu.SMEM)] * 2
        + [pl.BlockSpec(memory_space=pltpu.VMEM)] * len(pieces),
        out_specs=pl.BlockSpec(memory_space=pltpu.VMEM),
        compiler_params=pltpu.CompilerParams(vmem_limit_bytes=24 << 20),
        cost_estimate=pl.CostEstimate(flops=0, bytes_accessed=8 * height * width, transcendentals=0),
    )(pair, info, *pieces)


def order_kernel(place_ref, *refs):
    for offset, ref in enumerate(refs[:-1]):
        refs[-1][(place_ref[0] + offset) % 4] = ref[...]


def gather_x(part):
    behind = lax.ppermute(part, "col", X_SHIFT[1])
    ahead = lax.ppermute(part, "col", X_SHIFT[3])
    far = lax.ppermute(part, "col", X_SHIFT[2])
    return part, ahead, far, behind


def gather_core(ring, x):
    part = ring[0]
    mine = pl.pallas_call(
        order_kernel,
        out_shape=jax.ShapeDtypeStruct((4, *part.shape), part.dtype),
        in_specs=[pl.BlockSpec(memory_space=pltpu.SMEM)] + [pl.BlockSpec(memory_space=pltpu.VMEM)] * 4,
        out_specs=pl.BlockSpec(memory_space=pltpu.VMEM),
        compiler_params=pltpu.CompilerParams(vmem_limit_bytes=8 << 20),
        cost_estimate=pl.CostEstimate(flops=0, bytes_accessed=16 * part.size, transcendentals=0),
    )(x.reshape(1), *ring)
    return mine, lax.ppermute(mine, "col", CORE_SWAP)


def together(*values):
    return lax.optimization_barrier(values)


LINE = {
    sign: {step: [(i, i + sign) for i in line[:step]] for step in range(1, ROWS)}
    for sign, line in ((1, range(ROWS - 1)), (-1, range(ROWS - 1, 0, -1)))
}
ENDS_IN = LINE[1][1] + LINE[-1][1]
ENDS_OUT = [(2, 3), (1, 0)]


def scatter_row(compact, z, gates={}):
    quarters = compact.reshape(ROWS, -1, BLK)

    def own(index):
        return pick(quarters, jnp.clip(index, 0, ROWS - 1))

    def sender(got, index, here):
        return jnp.where(here, add(own(index), got), own(index).astype(F32)).astype(BF16)

    got = lax.ppermute(own(ROWS - 1 - z), "row", ENDS_IN)
    up, down = together(
        sender(got, z + 2, z == 1), sender(got, z - 2, z == 2), *gates.get(2, ())
    )[:2]
    up = lax.ppermute(up, "row", LINE[1][2])
    down = lax.ppermute(down, "row", LINE[-1][2])
    up, down = together(
        add(own(z + 1), up).astype(BF16), add(own(z - 1), down).astype(BF16), *gates.get(3, ())
    )[:2]
    up = lax.ppermute(up, "row", LINE[1][3])
    down = lax.ppermute(down, "row", LINE[-1][3])
    return add(own(z), up, down)


def gather_row(own, z, gates={}):
    below = lax.ppermute(own, "row", LINE[1][3])
    above = lax.ppermute(own, "row", LINE[-1][3])
    up, down = together(below, above, *gates.get(2, ()))[:2]
    below2 = lax.ppermute(up, "row", LINE[1][3][1:])
    above2 = lax.ppermute(down, "row", LINE[-1][3][1:])
    last = after(jnp.where(z == 2, below2, above2), *gates.get(3, ()))
    last = lax.ppermute(last, "row", ENDS_OUT)
    return [last, below2, below, own, above, above2, last]


def ring_first(stack, i, axis, forward, backward):
    rows = stack.shape[1] // 2
    far = pick(stack, (i + 2) % 4)
    return lax.ppermute(far[:rows], axis, forward), lax.ppermute(far[rows:], axis, backward)


def ring_second(stack, i, axis, forward, backward, first):
    rows = stack.shape[1] // 2
    right = pick(stack, (i + 1) % 4)
    left = pick(stack, (i + 3) % 4)
    right = jnp.concatenate([add(right[:rows], first[0]).astype(BF16), right[rows:]])
    left = jnp.concatenate([left[:rows], add(left[rows:], first[1]).astype(BF16)])
    return lax.ppermute(right, axis, forward), lax.ppermute(left, axis, backward)


def scatter_ring(stack, i, *ring):
    return add(pick(stack, i), *ring_second(stack, i, *ring, ring_first(stack, i, *ring)))


def y_parts(term):
    return term.reshape(4, term.shape[0] // 4, term.shape[1])


Y_RING = ("dp", Y_SHIFT[1], Y_SHIFT[3])


def scatter_half(part, half, scale):
    halves = part.reshape(2, part.shape[0] // 2, part.shape[1])
    got = lax.ppermute(pick(halves, 1 - half).astype(BF16), "dp", HALF_SWAP)
    return (add(pick(halves, half), got) * scale).astype(BF16)


def scatter_col(term, x, core):
    stack = term.reshape(4, 2, term.shape[0] // 8, term.shape[1])
    keep = lax.dynamic_index_in_dim(stack, core, 1, keepdims=False)
    give = lax.dynamic_index_in_dim(stack, 1 - core, 1, keepdims=False)
    chip = add(keep, lax.ppermute(give, "col", CORE_SWAP)).astype(BF16)
    return scatter_ring(chip, x, "col", X_SHIFT[1], X_SHIFT[3]).astype(BF16)


def contract(lhs, rhs, left, right):
    return lax.dot_general(
        lhs, rhs, (((left,), (right,)), ((), ())), preferred_element_type=F32
    ).astype(BF16)


def run(capacity, all_tokens, pre, grad_parts, in_weight, out_weight, active):
    dp, z, col = lax.axis_index("dp"), lax.axis_index("row"), lax.axis_index("col")
    y, half, x, core = dp // 2, dp % 2, col // 2, col % 2
    hidden_local = in_weight.shape[1]
    pair, count = make_slots(active, capacity)
    info = jnp.stack([z, count]).astype(jnp.int32)
    pre = compact(pair, pre)
    height, width = all_tokens.shape[0], all_tokens.shape[1] // 2
    scale = (height * lax.axis_size("dp")) ** (-0.5)
    all_grad, back = project(core, *grad_parts, out_weight, 1, pair)
    pre = scatter_row(pre, z, {2: (back,)})
    lifted = jax.nn.relu(pre)
    pieces = gather_row((lifted * lifted).astype(BF16), z)
    back = scatter_row(after(back, pieces[ROWS - 2], pieces[ROWS]), z)
    hidden_grad = (back * (2.0 * lifted)).astype(BF16)

    hidden = spread(pair, info, pieces, height, hidden_local)
    out_term = y_parts(contract(hidden, all_grad, 0, 0))
    first = ring_first(out_term, y, *Y_RING)
    pieces = gather_row(hidden_grad, z, {2: (out_term,), 3: first})
    second = ring_second(out_term, y, *Y_RING, first)
    pieces[0] = after(pieces[0], *second)
    hidden_grad = spread(pair, info, pieces, height, hidden_local)
    in_terms = [
        y_parts(contract(hidden_grad, cols, 0, 0))
        for cols in (all_tokens[:, :width], all_tokens[:, width:])
    ]
    out_part = after(add(pick(out_term, y), *second), *in_terms)
    out_weight_grad = scatter_half(out_part, half, scale)
    in_weight_grad = jnp.concatenate(
        [scatter_half(scatter_ring(term, y, *Y_RING), half, scale) for term in in_terms], axis=1
    )
    hidden_grad = after(hidden_grad, *in_terms)
    token_grad = scatter_col(contract(hidden_grad, in_weight, 1, 1), x, core)
    return (token_grad, in_weight_grad, out_weight_grad)


def body(tokens, out_grad, in_weight, out_weight, active_lists, active_counts):
    col = lax.axis_index("col")
    local_blocks = in_weight.shape[1] // BLK
    active = active_pairs(active_lists, active_counts, local_blocks * lax.axis_size("col"))
    most = most_pairs(active, local_blocks)
    active = lax.dynamic_slice_in_dim(active, col * local_blocks, local_blocks, 1)
    ring = gather_x(tokens)
    most, out_grad, *ring = together(most, out_grad, *ring)
    grad_ring = gather_x(out_grad)
    most = jnp.maximum(most, lax.ppermute(most, "dp", HALF_SWAP))
    all_tokens, pre = project(col % 2, *gather_core(ring, col // 2), in_weight, 0)
    grad_ring = (after(grad_ring[0], pre), *grad_ring[1:])
    grad_parts = gather_core((after(grad_ring[0], most), *grad_ring[1:]), col // 2)
    most = most[0, 0]
    fits = sum((most > capacity).astype(jnp.int32) for capacity in CAPACITIES)
    branches = [
        functools.partial(run, capacity) for capacity in (*CAPACITIES, active.shape[0] * local_blocks)
    ]
    return lax.switch(fits, branches, all_tokens, pre, grad_parts, in_weight, out_weight, active)


def solution(mesh):
    in_specs = (
        P(("dp", "col"), "row"),
        P(("dp", "col"), "row"),
        P("row", "col"),
        P("col", "row"),
        P("dp", None),
        P("dp"),
    )
    out_specs = (P(("dp", "col"), "row"), P(("col", "dp"), "row"), P(("col", "dp"), "row"))
    return jax.shard_map(body, mesh=mesh, in_specs=in_specs, out_specs=out_specs, check_vma=False)
```

```python
import functools

import jax
import jax.numpy as jnp
from jax import lax
from jax.experimental import pallas as pl
from jax.experimental.pallas import tpu as pltpu
from jax.sharding import PartitionSpec as P

BLK = 128
F32 = jnp.float32
BF16 = jnp.bfloat16
X_SHIFT = {s: [(c, ((c // 2 + s) % 4) * 2 + c % 2) for c in range(8)] for s in (1, 2, 3)}
CORE_SWAP = [(c, c ^ 1) for c in range(8)]
Y_SHIFT = {s: [(d, ((d // 2 + s) % 4) * 2 + d % 2) for d in range(8)] for s in (1, 2, 3)}
HALF_SWAP = [(d, d ^ 1) for d in range(8)]
ROWS = 4
CAPACITIES = (60,)


def pick(stack, index):
    return lax.dynamic_index_in_dim(stack, index, 0, keepdims=False)


def add(*terms):
    total = terms[0].astype(F32)
    for term in terms[1:]:
        total = total + term.astype(F32)
    return total


def after(value, *others):
    return lax.optimization_barrier((value, *others))[0]


def active_pairs(active_lists, active_counts, blocks):
    slots = jnp.arange(active_lists.shape[1], dtype=jnp.int32)
    valid = slots[None, :] < active_counts[:, None]
    wanted = jnp.arange(blocks, dtype=jnp.int32)
    hits = (active_lists[:, :, None] == wanted[None, None, :]) & valid[:, :, None]
    return jnp.any(hits, axis=1).astype(jnp.int32)


def most_pairs(active, local_blocks):
    groups = active.reshape(active.shape[0], -1, local_blocks)
    most = jnp.broadcast_to(jnp.max(jnp.sum(groups, axis=(0, 2))), (8, 128))
    for shift in (Y_SHIFT[1], Y_SHIFT[2]):
        most = jnp.maximum(most, lax.ppermute(most, "dp", shift))
    return most


def make_slots(active, capacity):
    active = active.reshape(-1)
    pairs = jnp.arange(active.shape[0], dtype=jnp.int32)
    before = jnp.sum(jnp.where(pairs[None, :] < pairs[:, None], active[None, :], 0), axis=1)
    place = jnp.where(active > 0, before, -1)
    want = jnp.arange(capacity, dtype=jnp.int32)
    pair = jnp.sum(jnp.where(place[None, :] == want[:, None], pairs[None, :], 0), axis=1)
    return pair, jnp.sum(active)


def join(core, mine_ref, other_ref, x_ref):
    chips, rows = mine_ref.shape[0], mine_ref.shape[1]
    for i in range(chips):
        for ref, at in ((mine_ref, 2 * i + core), (other_ref, 2 * i + 1 - core)):
            x_ref[pl.ds(pl.multiple_of(at * rows, rows), rows), :] = ref[i]


def multiply(rhs_dims, x_ref, w_ref, dense_ref):
    wide = 2 * BLK

    def one(n, carry):
        cols = pl.ds(pl.multiple_of(n * wide, wide), wide)
        w = w_ref[:, cols] if rhs_dims == 0 else w_ref[cols, :]
        dense_ref[:, cols] = lax.dot_general(
            x_ref[...], w, (((1,), (rhs_dims,)), ((), ())), preferred_element_type=F32
        ).astype(BF16)
        return carry

    lax.fori_loop(0, dense_ref.shape[1] // wide, one, 0)


def compact_kernel(pair_ref, dense_ref, out_ref):
    blocks = dense_ref.shape[1] // BLK

    def one(j, carry):
        pair = pair_ref[j]
        t = pl.multiple_of((pair // blocks) * BLK, BLK)
        f = pl.multiple_of((pair % blocks) * BLK, BLK)
        out_ref[pl.ds(pl.multiple_of(j * BLK, BLK), BLK), :] = dense_ref[pl.ds(t, BLK), pl.ds(f, BLK)]
        return carry

    lax.fori_loop(0, out_ref.shape[0] // BLK, one, 0)


def dense_kernel(rhs_dims, core_ref, mine_ref, other_ref, w_ref, x_ref, dense_ref):
    join(core_ref[0], mine_ref, other_ref, x_ref)
    multiply(rhs_dims, x_ref, w_ref, dense_ref)


def project_kernel(rhs_dims, pair_ref, core_ref, mine_ref, other_ref, w_ref, x_ref, out_ref, dense_ref):
    join(core_ref[0], mine_ref, other_ref, x_ref)
    multiply(rhs_dims, x_ref, w_ref, dense_ref)
    compact_kernel(pair_ref, dense_ref, out_ref)


def compact(pair, dense):
    shape = (pair.shape[0] * BLK, BLK)
    return pl.pallas_call(
        compact_kernel,
        out_shape=jax.ShapeDtypeStruct(shape, BF16),
        in_specs=[pl.BlockSpec(memory_space=pltpu.SMEM), pl.BlockSpec(memory_space=pltpu.VMEM)],
        out_specs=pl.BlockSpec(memory_space=pltpu.VMEM),
        compiler_params=pltpu.CompilerParams(vmem_limit_bytes=16 << 20),
        cost_estimate=pl.CostEstimate(
            flops=0, bytes_accessed=2 * (dense.size + shape[0] * BLK), transcendentals=0
        ),
    )(pair, dense)


def project(core, mine, other, w, rhs_dims, pair=None):
    depth = mine.shape[2]
    height = 2 * mine.shape[0] * mine.shape[1]
    width = w.shape[1 - rhs_dims]
    dense = (height, width)
    result = dense if pair is None else (pair.shape[0] * BLK, BLK)
    scalars = [core.reshape(1)] if pair is None else [pair, core.reshape(1)]
    return pl.pallas_call(
        functools.partial(dense_kernel if pair is None else project_kernel, rhs_dims),
        out_shape=(jax.ShapeDtypeStruct((height, depth), BF16), jax.ShapeDtypeStruct(result, BF16)),
        in_specs=[pl.BlockSpec(memory_space=pltpu.SMEM)] * len(scalars)
        + [pl.BlockSpec(memory_space=pltpu.VMEM)] * 3,
        out_specs=(pl.BlockSpec(memory_space=pltpu.VMEM), pl.BlockSpec(memory_space=pltpu.VMEM)),
        scratch_shapes=[] if pair is None else [pltpu.VMEM(dense, BF16)],
        compiler_params=pltpu.CompilerParams(vmem_limit_bytes=24 << 20),
        cost_estimate=pl.CostEstimate(
            flops=2 * height * depth * width,
            bytes_accessed=2 * (height * depth + depth * width + result[0] * result[1]),
            transcendentals=0,
        ),
    )(*scalars, mine, other, w)


def spread_kernel(blocks, share, pair_ref, info_ref, *refs):
    dense_ref = refs[-1]
    dense_ref[...] = jnp.zeros_like(dense_ref)
    place, count = info_ref[0], info_ref[1]
    piece = refs[0].shape[0] // BLK
    streams = share // piece
    for i, ref in enumerate(refs[:-1]):
        owner = place + i // streams + 1 - ROWS
        first = owner * share + (i % streams) * piece
        stop = jnp.where((owner >= 0) & (owner < ROWS), jnp.clip(count - first, 0, piece), 0)

        def one(j, carry, ref=ref, first=first):
            pair = pair_ref[first + j]
            t = pl.multiple_of((pair // blocks) * BLK, BLK)
            f = pl.multiple_of((pair % blocks) * BLK, BLK)
            dense_ref[pl.ds(t, BLK), pl.ds(f, BLK)] = ref[pl.ds(pl.multiple_of(j * BLK, BLK), BLK), :]
            return carry

        lax.fori_loop(0, stop, one, 0)


def spread(pair, info, pieces, height, width):
    return pl.pallas_call(
        functools.partial(spread_kernel, width // BLK, pair.shape[0] // ROWS),
        out_shape=jax.ShapeDtypeStruct((height, width), BF16),
        in_specs=[pl.BlockSpec(memory_space=pltpu.SMEM)] * 2
        + [pl.BlockSpec(memory_space=pltpu.VMEM)] * len(pieces),
        out_specs=pl.BlockSpec(memory_space=pltpu.VMEM),
        compiler_params=pltpu.CompilerParams(vmem_limit_bytes=24 << 20),
        cost_estimate=pl.CostEstimate(flops=0, bytes_accessed=8 * height * width, transcendentals=0),
    )(pair, info, *pieces)


def order_kernel(place_ref, *refs):
    for offset, ref in enumerate(refs[:-1]):
        refs[-1][(place_ref[0] + offset) % 4] = ref[...]


def gather_x(part):
    behind = lax.ppermute(part, "col", X_SHIFT[1])
    ahead = lax.ppermute(part, "col", X_SHIFT[3])
    far = lax.ppermute(part, "col", X_SHIFT[2])
    return part, ahead, far, behind


def gather_core(ring, x):
    part = ring[0]
    mine = pl.pallas_call(
        order_kernel,
        out_shape=jax.ShapeDtypeStruct((4, *part.shape), part.dtype),
        in_specs=[pl.BlockSpec(memory_space=pltpu.SMEM)] + [pl.BlockSpec(memory_space=pltpu.VMEM)] * 4,
        out_specs=pl.BlockSpec(memory_space=pltpu.VMEM),
        compiler_params=pltpu.CompilerParams(vmem_limit_bytes=8 << 20),
        cost_estimate=pl.CostEstimate(flops=0, bytes_accessed=16 * part.size, transcendentals=0),
    )(x.reshape(1), *ring)
    return mine, lax.ppermute(mine, "col", CORE_SWAP)


def together(*values):
    return lax.optimization_barrier(values)


LINE = {
    sign: {step: [(i, i + sign) for i in line[:step]] for step in range(1, ROWS)}
    for sign, line in ((1, range(ROWS - 1)), (-1, range(ROWS - 1, 0, -1)))
}
ENDS_IN = LINE[1][1] + LINE[-1][1]
ENDS_OUT = [(2, 3), (1, 0)]


def scatter_row(compact, z, gates={}):
    quarters = compact.reshape(ROWS, -1, BLK)

    def own(index):
        return pick(quarters, jnp.clip(index, 0, ROWS - 1))

    def sender(got, index, here):
        return jnp.where(here, add(own(index), got), own(index).astype(F32)).astype(BF16)

    got = lax.ppermute(own(ROWS - 1 - z), "row", ENDS_IN)
    up, down = together(
        sender(got, z + 2, z == 1), sender(got, z - 2, z == 2), *gates.get(2, ())
    )[:2]
    up = lax.ppermute(up, "row", LINE[1][2])
    down = lax.ppermute(down, "row", LINE[-1][2])
    up, down = together(
        add(own(z + 1), up).astype(BF16), add(own(z - 1), down).astype(BF16), *gates.get(3, ())
    )[:2]
    up = lax.ppermute(up, "row", LINE[1][3])
    down = lax.ppermute(down, "row", LINE[-1][3])
    return add(own(z), up, down)


def gather_row(own, z, gates={}):
    below = lax.ppermute(own, "row", LINE[1][3])
    above = lax.ppermute(own, "row", LINE[-1][3])
    up, down = together(below, above, *gates.get(2, ()))[:2]
    below2 = lax.ppermute(up, "row", LINE[1][3][1:])
    above2 = lax.ppermute(down, "row", LINE[-1][3][1:])
    last = after(jnp.where(z == 2, below2, above2), *gates.get(3, ()))
    last = lax.ppermute(last, "row", ENDS_OUT)
    return [last, below2, below, own, above, above2, last]


def ring_first(stack, i, axis, forward, backward):
    rows = stack.shape[1] // 2
    far = pick(stack, (i + 2) % 4)
    return lax.ppermute(far[:rows], axis, forward), lax.ppermute(far[rows:], axis, backward)


def ring_second(stack, i, axis, forward, backward, first):
    rows = stack.shape[1] // 2
    right = pick(stack, (i + 1) % 4)
    left = pick(stack, (i + 3) % 4)
    right = jnp.concatenate([add(right[:rows], first[0]).astype(BF16), right[rows:]])
    left = jnp.concatenate([left[:rows], add(left[rows:], first[1]).astype(BF16)])
    return lax.ppermute(right, axis, forward), lax.ppermute(left, axis, backward)


def scatter_ring(stack, i, *ring):
    return add(pick(stack, i), *ring_second(stack, i, *ring, ring_first(stack, i, *ring)))


def y_parts(term):
    return term.reshape(4, term.shape[0] // 4, term.shape[1])


Y_RING = ("dp", Y_SHIFT[1], Y_SHIFT[3])


def scatter_half(part, half, scale):
    halves = part.reshape(2, part.shape[0] // 2, part.shape[1])
    got = lax.ppermute(pick(halves, 1 - half).astype(BF16), "dp", HALF_SWAP)
    return (add(pick(halves, half), got) * scale).astype(BF16)


def scatter_col(term, x, core):
    stack = term.reshape(4, 2, term.shape[0] // 8, term.shape[1])
    keep = lax.dynamic_index_in_dim(stack, core, 1, keepdims=False)
    give = lax.dynamic_index_in_dim(stack, 1 - core, 1, keepdims=False)
    chip = add(keep, lax.ppermute(give, "col", CORE_SWAP)).astype(BF16)
    return scatter_ring(chip, x, "col", X_SHIFT[1], X_SHIFT[3]).astype(BF16)


def contract(lhs, rhs, left, right):
    return lax.dot_general(
        lhs, rhs, (((left,), (right,)), ((), ())), preferred_element_type=F32
    ).astype(BF16)


def run(capacity, all_tokens, pre, grad_parts, in_weight, out_weight, active):
    dp, z, col = lax.axis_index("dp"), lax.axis_index("row"), lax.axis_index("col")
    y, half, x, core = dp // 2, dp % 2, col // 2, col % 2
    hidden_local = in_weight.shape[1]
    pair, count = make_slots(active, capacity)
    info = jnp.stack([z, count]).astype(jnp.int32)
    pre = compact(pair, pre)
    height, width = all_tokens.shape[0], all_tokens.shape[1] // 2
    scale = (height * lax.axis_size("dp")) ** (-0.5)
    all_grad, back = project(core, *grad_parts, out_weight, 1, pair)
    pre = scatter_row(pre, z, {2: (back,)})
    lifted = jax.nn.relu(pre)
    pieces = gather_row((lifted * lifted).astype(BF16), z)
    back = scatter_row(after(back, pieces[ROWS - 2], pieces[ROWS]), z)
    hidden_grad = (back * (2.0 * lifted)).astype(BF16)

    hidden = spread(pair, info, pieces, height, hidden_local)
    out_term = y_parts(contract(hidden, all_grad, 0, 0))
    first = ring_first(out_term, y, *Y_RING)
    pieces = gather_row(hidden_grad, z, {2: (out_term,), 3: first})
    second = ring_second(out_term, y, *Y_RING, first)
    pieces[0] = after(pieces[0], *second)
    hidden_grad = spread(pair, info, pieces, height, hidden_local)
    in_terms = [
        y_parts(contract(hidden_grad, cols, 0, 0))
        for cols in (all_tokens[:, :width], all_tokens[:, width:])
    ]
    firsts = [ring_first(term, y, *Y_RING) for term in in_terms]
    out_part = after(add(pick(out_term, y), *second), *firsts[0], *firsts[1])
    out_weight_grad = scatter_half(out_part, half, scale)
    in_parts = [
        add(pick(term, y), *ring_second(term, y, *Y_RING, first))
        for term, first in zip(in_terms, firsts)
    ]
    in_weight_grad = jnp.concatenate([scatter_half(part, half, scale) for part in in_parts], axis=1)
    hidden_grad = after(hidden_grad, *in_terms)
    token_grad = scatter_col(contract(hidden_grad, in_weight, 1, 1), x, core)
    return (token_grad, in_weight_grad, out_weight_grad)


def ring_sum(parts, axis):
    n = parts.shape[0]
    i = lax.axis_index(axis)
    ring = [(j, (j + 1) % n) for j in range(n)]

    def hop(step, total):
        return add(pick(parts, (i + 2 * n - 2 - step) % n), lax.ppermute(total, axis, ring)).astype(BF16)

    return lax.fori_loop(0, n - 1, hop, pick(parts, (i + n - 1) % n))


def run_all(all_tokens, pre, grad_parts, in_weight, out_weight, active):
    core = lax.axis_index("col") % 2
    all_grad, back = project(core, *grad_parts, out_weight, 1)
    ring = [(j, (j + 1) % ROWS) for j in range(ROWS)]

    def hop(step, carry):
        sent, total = carry
        sent = lax.ppermute(sent, "row", ring)
        return sent, add(total, sent)

    sent = jnp.stack([pre, back])
    pre, back = lax.fori_loop(0, ROWS - 1, hop, (sent, sent.astype(F32)))[1]
    mask = jnp.repeat(jnp.repeat(active.astype(F32), BLK, axis=0), BLK, axis=1)
    lifted = jax.nn.relu(pre) * mask
    hidden = (lifted * lifted).astype(BF16)
    hidden_grad = (back * (2.0 * lifted)).astype(BF16)
    height, width = all_tokens.shape
    scale = (height * lax.axis_size("dp")) ** (-0.5)
    terms = [contract(hidden_grad, all_tokens, 0, 0), contract(hidden, all_grad, 0, 0)]
    both = jnp.concatenate(terms, axis=1).reshape(lax.axis_size("dp"), -1, 2 * width)
    both = (ring_sum(both, "dp").astype(F32) * scale).astype(BF16)
    token_grad = contract(hidden_grad, in_weight, 1, 1).reshape(lax.axis_size("col"), -1, width)
    return ring_sum(token_grad, "col"), both[:, :width], both[:, width:]


def body(tokens, out_grad, in_weight, out_weight, active_lists, active_counts):
    col = lax.axis_index("col")
    local_blocks = in_weight.shape[1] // BLK
    active = active_pairs(active_lists, active_counts, local_blocks * lax.axis_size("col"))
    most = most_pairs(active, local_blocks)
    active = lax.dynamic_slice_in_dim(active, col * local_blocks, local_blocks, 1)
    ring = gather_x(tokens)
    most, out_grad, *ring = together(most, out_grad, *ring)
    grad_ring = gather_x(out_grad)
    all_tokens, pre = project(col % 2, *gather_core(ring, col // 2), in_weight, 0)
    most, *grad_ring = together(most, *grad_ring, pre)[:5]
    grad_parts = gather_core(grad_ring, col // 2)
    most = jnp.maximum(most, lax.ppermute(most, "dp", HALF_SWAP))[0, 0]
    fits = sum((most > capacity).astype(jnp.int32) for capacity in CAPACITIES)
    branches = [functools.partial(run, capacity) for capacity in CAPACITIES] + [run_all]
    return lax.switch(fits, branches, all_tokens, pre, grad_parts, in_weight, out_weight, active)


def solution(mesh):
    in_specs = (
        P(("dp", "col"), "row"),
        P(("dp", "col"), "row"),
        P("row", "col"),
        P("col", "row"),
        P("dp", None),
        P("dp"),
    )
    out_specs = (P(("dp", "col"), "row"), P(("col", "dp"), "row"), P(("col", "dp"), "row"))
    return jax.shard_map(body, mesh=mesh, in_specs=in_specs, out_specs=out_specs, check_vma=False)
```

```python
import functools

import jax
import jax.numpy as jnp
from jax import lax
from jax.experimental import pallas as pl
from jax.experimental.pallas import tpu as pltpu
from jax.sharding import PartitionSpec as P

BLK = 128
F32 = jnp.float32
BF16 = jnp.bfloat16
X_SHIFT = {s: [(c, ((c // 2 + s) % 4) * 2 + c % 2) for c in range(8)] for s in (1, 2, 3)}
CORE_SWAP = [(c, c ^ 1) for c in range(8)]
Y_SHIFT = {s: [(d, ((d // 2 + s) % 4) * 2 + d % 2) for d in range(8)] for s in (1, 2, 3)}
HALF_SWAP = [(d, d ^ 1) for d in range(8)]
ROWS = 4
CAPACITIES = (56,)


def pick(stack, index):
    return lax.dynamic_index_in_dim(stack, index, 0, keepdims=False)


def add(*terms):
    total = terms[0].astype(F32)
    for term in terms[1:]:
        total = total + term.astype(F32)
    return total


def after(value, *others):
    return lax.optimization_barrier((value, *others))[0]


def active_pairs(active_lists, active_counts, blocks):
    slots = jnp.arange(active_lists.shape[1], dtype=jnp.int32)
    valid = slots[None, :] < active_counts[:, None]
    wanted = jnp.arange(blocks, dtype=jnp.int32)
    hits = (active_lists[:, :, None] == wanted[None, None, :]) & valid[:, :, None]
    return jnp.any(hits, axis=1).astype(jnp.int32)


def most_pairs(active, local_blocks):
    groups = active.reshape(active.shape[0], -1, local_blocks)
    most = jnp.broadcast_to(jnp.max(jnp.sum(groups, axis=(0, 2))), (8, 128))
    for shift in (Y_SHIFT[1], Y_SHIFT[2]):
        most = jnp.maximum(most, lax.ppermute(most, "dp", shift))
    return most


def make_slots(active, capacity):
    active = active.reshape(-1)
    pairs = jnp.arange(active.shape[0], dtype=jnp.int32)
    before = jnp.sum(jnp.where(pairs[None, :] < pairs[:, None], active[None, :], 0), axis=1)
    place = jnp.where(active > 0, before, -1)
    want = jnp.arange(capacity, dtype=jnp.int32)
    pair = jnp.sum(jnp.where(place[None, :] == want[:, None], pairs[None, :], 0), axis=1)
    return pair, jnp.sum(active)


def project_kernel(rhs_dims, blocks, pair_ref, core_ref, mine_ref, other_ref, w_ref, out_ref, x_ref, dense_ref):
    chips, rows = mine_ref.shape[0], mine_ref.shape[1]
    core = core_ref[0]
    for i in range(chips):
        for ref, at in ((mine_ref, 2 * i + core), (other_ref, 2 * i + 1 - core)):
            x_ref[pl.ds(pl.multiple_of(at * rows, rows), rows), :] = ref[i]
    wide = 2 * BLK
    for n in range(blocks // 2):
        cols = slice(n * wide, (n + 1) * wide)
        w = w_ref[:, cols] if rhs_dims == 0 else w_ref[cols, :]
        dense_ref[:, cols] = lax.dot_general(
            x_ref[...], w, (((1,), (rhs_dims,)), ((), ())), preferred_element_type=F32
        ).astype(BF16)

    def one(j, carry):
        pair = pair_ref[j]
        t = pl.multiple_of((pair // blocks) * BLK, BLK)
        f = pl.multiple_of((pair % blocks) * BLK, BLK)
        out_ref[pl.ds(pl.multiple_of(j * BLK, BLK), BLK), :] = dense_ref[pl.ds(t, BLK), pl.ds(f, BLK)]
        return carry

    lax.fori_loop(0, out_ref.shape[0] // BLK, one, 0)


def project(pair, core, mine, other, w, rhs_dims):
    depth = mine.shape[2]
    height = 2 * mine.shape[0] * mine.shape[1]
    width = w.shape[1 - rhs_dims]
    slots = pair.shape[0]
    return pl.pallas_call(
        functools.partial(project_kernel, rhs_dims, width // BLK),
        out_shape=(
            jax.ShapeDtypeStruct((slots * BLK, BLK), BF16),
            jax.ShapeDtypeStruct((height, depth), BF16),
        ),
        in_specs=[pl.BlockSpec(memory_space=pltpu.SMEM)] * 2
        + [pl.BlockSpec(memory_space=pltpu.VMEM)] * 3,
        out_specs=(pl.BlockSpec(memory_space=pltpu.VMEM), pl.BlockSpec(memory_space=pltpu.VMEM)),
        scratch_shapes=[pltpu.VMEM((height, width), BF16)],
        compiler_params=pltpu.CompilerParams(vmem_limit_bytes=24 << 20),
        cost_estimate=pl.CostEstimate(
            flops=2 * height * depth * width,
            bytes_accessed=2 * (height * depth + depth * width + slots * BLK * BLK),
            transcendentals=0,
        ),
    )(pair, core.reshape(1), mine, other, w)


def spread_kernel(blocks, share, pair_ref, info_ref, *refs):
    dense_ref = refs[-1]
    dense_ref[...] = jnp.zeros_like(dense_ref)
    place, count = info_ref[0], info_ref[1]
    piece = refs[0].shape[0] // BLK
    streams = share // piece
    for i, ref in enumerate(refs[:-1]):
        owner = place + i // streams + 1 - ROWS
        first = owner * share + (i % streams) * piece
        stop = jnp.where((owner >= 0) & (owner < ROWS), jnp.clip(count - first, 0, piece), 0)

        def one(j, carry, ref=ref, first=first):
            pair = pair_ref[first + j]
            t = pl.multiple_of((pair // blocks) * BLK, BLK)
            f = pl.multiple_of((pair % blocks) * BLK, BLK)
            dense_ref[pl.ds(t, BLK), pl.ds(f, BLK)] = ref[pl.ds(pl.multiple_of(j * BLK, BLK), BLK), :]
            return carry

        lax.fori_loop(0, stop, one, 0)


def spread(pair, info, pieces, height, width):
    return pl.pallas_call(
        functools.partial(spread_kernel, width // BLK, pair.shape[0] // ROWS),
        out_shape=jax.ShapeDtypeStruct((height, width), BF16),
        in_specs=[pl.BlockSpec(memory_space=pltpu.SMEM)] * 2
        + [pl.BlockSpec(memory_space=pltpu.VMEM)] * len(pieces),
        out_specs=pl.BlockSpec(memory_space=pltpu.VMEM),
        compiler_params=pltpu.CompilerParams(vmem_limit_bytes=24 << 20),
        cost_estimate=pl.CostEstimate(flops=0, bytes_accessed=8 * height * width, transcendentals=0),
    )(pair, info, *pieces)


def order_kernel(place_ref, *refs):
    for offset, ref in enumerate(refs[:-1]):
        refs[-1][(place_ref[0] + offset) % 4] = ref[...]


def gather_x(part):
    behind = lax.ppermute(part, "col", X_SHIFT[1])
    ahead = lax.ppermute(part, "col", X_SHIFT[3])
    far = lax.ppermute(part, "col", X_SHIFT[2])
    return part, ahead, far, behind


def gather_core(ring, x):
    part = ring[0]
    mine = pl.pallas_call(
        order_kernel,
        out_shape=jax.ShapeDtypeStruct((4, *part.shape), part.dtype),
        in_specs=[pl.BlockSpec(memory_space=pltpu.SMEM)] + [pl.BlockSpec(memory_space=pltpu.VMEM)] * 4,
        out_specs=pl.BlockSpec(memory_space=pltpu.VMEM),
        compiler_params=pltpu.CompilerParams(vmem_limit_bytes=8 << 20),
        cost_estimate=pl.CostEstimate(flops=0, bytes_accessed=16 * part.size, transcendentals=0),
    )(x.reshape(1), *ring)
    return mine, lax.ppermute(mine, "col", CORE_SWAP)


def together(*values):
    return lax.optimization_barrier(values)


LINE = {
    sign: {step: [(i, i + sign) for i in line[:step]] for step in range(1, ROWS)}
    for sign, line in ((1, range(ROWS - 1)), (-1, range(ROWS - 1, 0, -1)))
}
ENDS_IN = LINE[1][1] + LINE[-1][1]
ENDS_OUT = [(2, 3), (1, 0)]


def scatter_row(compact, z, gates={}):
    quarters = compact.reshape(ROWS, -1, BLK)

    def own(index):
        return pick(quarters, jnp.clip(index, 0, ROWS - 1))

    def sender(got, index, here):
        return jnp.where(here, add(own(index), got), own(index).astype(F32)).astype(BF16)

    got = lax.ppermute(own(ROWS - 1 - z), "row", ENDS_IN)
    up, down = together(
        sender(got, z + 2, z == 1), sender(got, z - 2, z == 2), *gates.get(2, ())
    )[:2]
    up = lax.ppermute(up, "row", LINE[1][2])
    down = lax.ppermute(down, "row", LINE[-1][2])
    up, down = together(
        add(own(z + 1), up).astype(BF16), add(own(z - 1), down).astype(BF16), *gates.get(3, ())
    )[:2]
    up = lax.ppermute(up, "row", LINE[1][3])
    down = lax.ppermute(down, "row", LINE[-1][3])
    return add(own(z), up, down)


def gather_row(own, z, gates={}):
    below = lax.ppermute(own, "row", LINE[1][3])
    above = lax.ppermute(own, "row", LINE[-1][3])
    up, down = together(below, above, *gates.get(2, ()))[:2]
    below2 = lax.ppermute(up, "row", LINE[1][3][1:])
    above2 = lax.ppermute(down, "row", LINE[-1][3][1:])
    last = after(jnp.where(z == 2, below2, above2), *gates.get(3, ()))
    last = lax.ppermute(last, "row", ENDS_OUT)
    return [last, below2, below, own, above, above2, last]


def ring_first(stack, i, axis, forward, backward):
    rows = stack.shape[1] // 2
    far = pick(stack, (i + 2) % 4)
    return lax.ppermute(far[:rows], axis, forward), lax.ppermute(far[rows:], axis, backward)


def ring_second(stack, i, axis, forward, backward, first):
    rows = stack.shape[1] // 2
    right = pick(stack, (i + 1) % 4)
    left = pick(stack, (i + 3) % 4)
    right = jnp.concatenate([add(right[:rows], first[0]).astype(BF16), right[rows:]])
    left = jnp.concatenate([left[:rows], add(left[rows:], first[1]).astype(BF16)])
    return lax.ppermute(right, axis, forward), lax.ppermute(left, axis, backward)


def scatter_ring(stack, i, *ring):
    return add(pick(stack, i), *ring_second(stack, i, *ring, ring_first(stack, i, *ring)))


def y_parts(term):
    return term.reshape(4, term.shape[0] // 4, term.shape[1])


Y_RING = ("dp", Y_SHIFT[1], Y_SHIFT[3])


def scatter_half(part, half, scale):
    halves = part.reshape(2, part.shape[0] // 2, part.shape[1])
    got = lax.ppermute(pick(halves, 1 - half).astype(BF16), "dp", HALF_SWAP)
    return (add(pick(halves, half), got) * scale).astype(BF16)


def scatter_col(term, x, core):
    stack = term.reshape(4, 2, term.shape[0] // 8, term.shape[1])
    keep = lax.dynamic_index_in_dim(stack, core, 1, keepdims=False)
    give = lax.dynamic_index_in_dim(stack, 1 - core, 1, keepdims=False)
    chip = add(keep, lax.ppermute(give, "col", CORE_SWAP)).astype(BF16)
    return scatter_ring(chip, x, "col", X_SHIFT[1], X_SHIFT[3]).astype(BF16)


def contract(lhs, rhs, left, right):
    return lax.dot_general(
        lhs, rhs, (((left,), (right,)), ((), ())), preferred_element_type=F32
    ).astype(BF16)


def run(capacity, token_parts, grad_parts, in_weight, out_weight, active):
    dp, z, col = lax.axis_index("dp"), lax.axis_index("row"), lax.axis_index("col")
    y, half, x, core = dp // 2, dp % 2, col // 2, col % 2
    hidden_local = in_weight.shape[1]
    pair, count = make_slots(active, capacity)
    info = jnp.stack([z, count]).astype(jnp.int32)
    pre, all_tokens = project(pair, core, *token_parts, in_weight, 0)
    height, width = all_tokens.shape[0], all_tokens.shape[1] // 2
    scale = (height * lax.axis_size("dp")) ** (-0.5)
    back, all_grad = project(pair, core, *grad_parts, out_weight, 1)
    pre = scatter_row(pre, z, {2: (back,)})
    lifted = jax.nn.relu(pre)
    pieces = gather_row((lifted * lifted).astype(BF16), z)
    back = scatter_row(after(back, pieces[ROWS - 2], pieces[ROWS]), z)
    hidden_grad = (back * (2.0 * lifted)).astype(BF16)

    hidden = spread(pair, info, pieces, height, hidden_local)
    out_term = y_parts(contract(hidden, all_grad, 0, 0))
    first = ring_first(out_term, y, *Y_RING)
    pieces = gather_row(hidden_grad, z, {2: (out_term,), 3: first})
    second = ring_second(out_term, y, *Y_RING, first)
    pieces[0] = after(pieces[0], *second)
    hidden_grad = spread(pair, info, pieces, height, hidden_local)
    in_terms = [
        y_parts(contract(hidden_grad, cols, 0, 0))
        for cols in (all_tokens[:, :width], all_tokens[:, width:])
    ]
    firsts = [ring_first(term, y, *Y_RING) for term in in_terms]
    out_part = after(add(pick(out_term, y), *second), *firsts[0])
    out_weight_grad = scatter_half(out_part, half, scale)
    in_parts = [
        add(pick(term, y), *ring_second(term, y, *Y_RING, first))
        for term, first in zip(in_terms, firsts)
    ]
    in_weight_grad = jnp.concatenate(
        [scatter_half(after(part, out_weight_grad), half, scale) for part in in_parts], axis=1
    )
    hidden_grad = after(hidden_grad, *in_terms)
    token_grad = scatter_col(contract(hidden_grad, in_weight, 1, 1), x, core)
    return (token_grad, in_weight_grad, out_weight_grad)


def body(tokens, out_grad, in_weight, out_weight, active_lists, active_counts):
    col = lax.axis_index("col")
    local_blocks = in_weight.shape[1] // BLK
    active = active_pairs(active_lists, active_counts, local_blocks * lax.axis_size("col"))
    most = most_pairs(active, local_blocks)
    active = lax.dynamic_slice_in_dim(active, col * local_blocks, local_blocks, 1)
    ring = gather_x(tokens)
    most, out_grad = together(most, out_grad, *ring[1:])[:2]
    grad_ring = gather_x(out_grad)
    most = jnp.maximum(most, lax.ppermute(most, "dp", HALF_SWAP))
    token_parts = gather_core(ring, col // 2)
    grad_parts = gather_core((after(grad_ring[0], most), *grad_ring[1:]), col // 2)
    most = most[0, 0]
    fits = sum((most > capacity).astype(jnp.int32) for capacity in CAPACITIES)
    branches = [
        functools.partial(run, capacity) for capacity in (*CAPACITIES, active.shape[0] * local_blocks)
    ]
    return lax.switch(fits, branches, token_parts, grad_parts, in_weight, out_weight, active)


def solution(mesh):
    in_specs = (
        P(("dp", "col"), "row"),
        P(("dp", "col"), "row"),
        P("row", "col"),
        P("col", "row"),
        P("dp", None),
        P("dp"),
    )
    out_specs = (P(("dp", "col"), "row"), P(("col", "dp"), "row"), P(("col", "dp"), "row"))
    return jax.shard_map(body, mesh=mesh, in_specs=in_specs, out_specs=out_specs, check_vma=False)
```

```python
import functools

import jax
import jax.numpy as jnp
from jax import lax
from jax.experimental import pallas as pl
from jax.experimental.pallas import tpu as pltpu
from jax.sharding import PartitionSpec as P

BLK = 128
F32 = jnp.float32
BF16 = jnp.bfloat16
X_SHIFT = {s: [(c, ((c // 2 + s) % 4) * 2 + c % 2) for c in range(8)] for s in (1, 2, 3)}
CORE_SWAP = [(c, c ^ 1) for c in range(8)]
Y_SHIFT = {s: [(d, ((d // 2 + s) % 4) * 2 + d % 2) for d in range(8)] for s in (1, 2, 3)}
HALF_SWAP = [(d, d ^ 1) for d in range(8)]
ROWS = 4
CAPACITIES = (56,)


def pick(stack, index):
    return lax.dynamic_index_in_dim(stack, index, 0, keepdims=False)


def add(*terms):
    total = terms[0].astype(F32)
    for term in terms[1:]:
        total = total + term.astype(F32)
    return total


def after(value, *others):
    return lax.optimization_barrier((value, *others))[0]


def active_pairs(active_lists, active_counts, blocks):
    slots = jnp.arange(active_lists.shape[1], dtype=jnp.int32)
    valid = slots[None, :] < active_counts[:, None]
    wanted = jnp.arange(blocks, dtype=jnp.int32)
    hits = (active_lists[:, :, None] == wanted[None, None, :]) & valid[:, :, None]
    return jnp.any(hits, axis=1).astype(jnp.int32)


def most_pairs(active, local_blocks):
    groups = active.reshape(active.shape[0], -1, local_blocks)
    most = jnp.broadcast_to(jnp.max(jnp.sum(groups, axis=(0, 2))), (8, 128))
    for shift in (Y_SHIFT[1], Y_SHIFT[2]):
        most = jnp.maximum(most, lax.ppermute(most, "dp", shift))
    return most


def make_slots(active, capacity):
    active = active.reshape(-1)
    pairs = jnp.arange(active.shape[0], dtype=jnp.int32)
    before = jnp.sum(jnp.where(pairs[None, :] < pairs[:, None], active[None, :], 0), axis=1)
    place = jnp.where(active > 0, before, -1)
    want = jnp.arange(capacity, dtype=jnp.int32)
    pair = jnp.sum(jnp.where(place[None, :] == want[:, None], pairs[None, :], 0), axis=1)
    return pair, jnp.sum(active)


def project_kernel(rhs_dims, blocks, pair_ref, core_ref, mine_ref, other_ref, w_ref, out_ref, x_ref, dense_ref):
    chips, rows = mine_ref.shape[0], mine_ref.shape[1]
    core = core_ref[0]
    for i in range(chips):
        for ref, at in ((mine_ref, 2 * i + core), (other_ref, 2 * i + 1 - core)):
            x_ref[pl.ds(pl.multiple_of(at * rows, rows), rows), :] = ref[i]
    wide = 2 * BLK
    for n in range(blocks // 2):
        cols = slice(n * wide, (n + 1) * wide)
        w = w_ref[:, cols] if rhs_dims == 0 else w_ref[cols, :]
        dense_ref[:, cols] = lax.dot_general(
            x_ref[...], w, (((1,), (rhs_dims,)), ((), ())), preferred_element_type=F32
        ).astype(BF16)

    def one(j, carry):
        pair = pair_ref[j]
        t = pl.multiple_of((pair // blocks) * BLK, BLK)
        f = pl.multiple_of((pair % blocks) * BLK, BLK)
        out_ref[pl.ds(pl.multiple_of(j * BLK, BLK), BLK), :] = dense_ref[pl.ds(t, BLK), pl.ds(f, BLK)]
        return carry

    lax.fori_loop(0, out_ref.shape[0] // BLK, one, 0)


def project(pair, core, mine, other, w, rhs_dims):
    depth = mine.shape[2]
    height = 2 * mine.shape[0] * mine.shape[1]
    width = w.shape[1 - rhs_dims]
    slots = pair.shape[0]
    return pl.pallas_call(
        functools.partial(project_kernel, rhs_dims, width // BLK),
        out_shape=(
            jax.ShapeDtypeStruct((slots * BLK, BLK), BF16),
            jax.ShapeDtypeStruct((height, depth), BF16),
        ),
        in_specs=[pl.BlockSpec(memory_space=pltpu.SMEM)] * 2
        + [pl.BlockSpec(memory_space=pltpu.VMEM)] * 3,
        out_specs=(pl.BlockSpec(memory_space=pltpu.VMEM), pl.BlockSpec(memory_space=pltpu.VMEM)),
        scratch_shapes=[pltpu.VMEM((height, width), BF16)],
        compiler_params=pltpu.CompilerParams(vmem_limit_bytes=24 << 20),
        cost_estimate=pl.CostEstimate(
            flops=2 * height * depth * width,
            bytes_accessed=2 * (height * depth + depth * width + slots * BLK * BLK),
            transcendentals=0,
        ),
    )(pair, core.reshape(1), mine, other, w)


def spread_kernel(blocks, share, pair_ref, info_ref, *refs):
    dense_ref = refs[-1]
    dense_ref[...] = jnp.zeros_like(dense_ref)
    place, count = info_ref[0], info_ref[1]
    piece = refs[0].shape[0] // BLK
    streams = share // piece
    for i, ref in enumerate(refs[:-1]):
        owner = place + i // streams + 1 - ROWS
        first = owner * share + (i % streams) * piece
        stop = jnp.where((owner >= 0) & (owner < ROWS), jnp.clip(count - first, 0, piece), 0)

        def one(j, carry, ref=ref, first=first):
            pair = pair_ref[first + j]
            t = pl.multiple_of((pair // blocks) * BLK, BLK)
            f = pl.multiple_of((pair % blocks) * BLK, BLK)
            dense_ref[pl.ds(t, BLK), pl.ds(f, BLK)] = ref[pl.ds(pl.multiple_of(j * BLK, BLK), BLK), :]
            return carry

        lax.fori_loop(0, stop, one, 0)


def spread(pair, info, pieces, height, width):
    return pl.pallas_call(
        functools.partial(spread_kernel, width // BLK, pair.shape[0] // ROWS),
        out_shape=jax.ShapeDtypeStruct((height, width), BF16),
        in_specs=[pl.BlockSpec(memory_space=pltpu.SMEM)] * 2
        + [pl.BlockSpec(memory_space=pltpu.VMEM)] * len(pieces),
        out_specs=pl.BlockSpec(memory_space=pltpu.VMEM),
        compiler_params=pltpu.CompilerParams(vmem_limit_bytes=24 << 20),
        cost_estimate=pl.CostEstimate(flops=0, bytes_accessed=8 * height * width, transcendentals=0),
    )(pair, info, *pieces)


def order_kernel(place_ref, *refs):
    for offset, ref in enumerate(refs[:-1]):
        refs[-1][(place_ref[0] + offset) % 4] = ref[...]


def gather_x(part):
    behind = lax.ppermute(part, "col", X_SHIFT[1])
    ahead = lax.ppermute(part, "col", X_SHIFT[3])
    far = lax.ppermute(part, "col", X_SHIFT[2])
    return part, ahead, far, behind


def gather_core(ring, x):
    part = ring[0]
    mine = pl.pallas_call(
        order_kernel,
        out_shape=jax.ShapeDtypeStruct((4, *part.shape), part.dtype),
        in_specs=[pl.BlockSpec(memory_space=pltpu.SMEM)] + [pl.BlockSpec(memory_space=pltpu.VMEM)] * 4,
        out_specs=pl.BlockSpec(memory_space=pltpu.VMEM),
        compiler_params=pltpu.CompilerParams(vmem_limit_bytes=8 << 20),
        cost_estimate=pl.CostEstimate(flops=0, bytes_accessed=16 * part.size, transcendentals=0),
    )(x.reshape(1), *ring)
    return mine, lax.ppermute(mine, "col", CORE_SWAP)


def together(*values):
    return lax.optimization_barrier(values)


LINE = {
    sign: {step: [(i, i + sign) for i in line[:step]] for step in range(1, ROWS)}
    for sign, line in ((1, range(ROWS - 1)), (-1, range(ROWS - 1, 0, -1)))
}
ENDS_IN = LINE[1][1] + LINE[-1][1]
ENDS_OUT = [(2, 3), (1, 0)]


def scatter_row(compact, z, gates={}):
    quarters = compact.reshape(ROWS, -1, BLK)

    def own(index):
        return pick(quarters, jnp.clip(index, 0, ROWS - 1))

    def sender(got, index, here):
        return jnp.where(here, add(own(index), got), own(index).astype(F32)).astype(BF16)

    got = lax.ppermute(own(ROWS - 1 - z), "row", ENDS_IN)
    up, down = together(
        sender(got, z + 2, z == 1), sender(got, z - 2, z == 2), *gates.get(2, ())
    )[:2]
    up = lax.ppermute(up, "row", LINE[1][2])
    down = lax.ppermute(down, "row", LINE[-1][2])
    up, down = together(
        add(own(z + 1), up).astype(BF16), add(own(z - 1), down).astype(BF16), *gates.get(3, ())
    )[:2]
    up = lax.ppermute(up, "row", LINE[1][3])
    down = lax.ppermute(down, "row", LINE[-1][3])
    return add(own(z), up, down)


def gather_row(own, z, gates={}):
    below = lax.ppermute(own, "row", LINE[1][3])
    above = lax.ppermute(own, "row", LINE[-1][3])
    up, down = together(below, above, *gates.get(2, ()))[:2]
    below2 = lax.ppermute(up, "row", LINE[1][3][1:])
    above2 = lax.ppermute(down, "row", LINE[-1][3][1:])
    last = after(jnp.where(z == 2, below2, above2), *gates.get(3, ()))
    last = lax.ppermute(last, "row", ENDS_OUT)
    return [last, below2, below, own, above, above2, last]


def ring_first(stack, i, axis, forward, backward):
    rows = stack.shape[1] // 2
    far = pick(stack, (i + 2) % 4)
    return lax.ppermute(far[:rows], axis, forward), lax.ppermute(far[rows:], axis, backward)


def ring_second(stack, i, axis, forward, backward, first):
    rows = stack.shape[1] // 2
    right = pick(stack, (i + 1) % 4)
    left = pick(stack, (i + 3) % 4)
    right = jnp.concatenate([add(right[:rows], first[0]).astype(BF16), right[rows:]])
    left = jnp.concatenate([left[:rows], add(left[rows:], first[1]).astype(BF16)])
    return lax.ppermute(right, axis, forward), lax.ppermute(left, axis, backward)


def scatter_ring(stack, i, *ring):
    return add(pick(stack, i), *ring_second(stack, i, *ring, ring_first(stack, i, *ring)))


def y_parts(term):
    return term.reshape(4, term.shape[0] // 4, term.shape[1])


Y_RING = ("dp", Y_SHIFT[1], Y_SHIFT[3])


def scatter_half(part, half, scale):
    halves = part.reshape(2, part.shape[0] // 2, part.shape[1])
    got = lax.ppermute(pick(halves, 1 - half).astype(BF16), "dp", HALF_SWAP)
    return (add(pick(halves, half), got) * scale).astype(BF16)


def scatter_col(term, x, core):
    stack = term.reshape(4, 2, term.shape[0] // 8, term.shape[1])
    keep = lax.dynamic_index_in_dim(stack, core, 1, keepdims=False)
    give = lax.dynamic_index_in_dim(stack, 1 - core, 1, keepdims=False)
    chip = add(keep, lax.ppermute(give, "col", CORE_SWAP)).astype(BF16)
    return scatter_ring(chip, x, "col", X_SHIFT[1], X_SHIFT[3]).astype(BF16)


def contract(lhs, rhs, left, right):
    return lax.dot_general(
        lhs, rhs, (((left,), (right,)), ((), ())), preferred_element_type=F32
    ).astype(BF16)


def run(capacity, token_parts, grad_parts, in_weight, out_weight, active):
    dp, z, col = lax.axis_index("dp"), lax.axis_index("row"), lax.axis_index("col")
    y, half, x, core = dp // 2, dp % 2, col // 2, col % 2
    hidden_local = in_weight.shape[1]
    pair, count = make_slots(active, capacity)
    info = jnp.stack([z, count]).astype(jnp.int32)
    pre, all_tokens = project(pair, core, *token_parts, in_weight, 0)
    height, width = all_tokens.shape[0], all_tokens.shape[1] // 2
    scale = (height * lax.axis_size("dp")) ** (-0.5)
    back, all_grad = project(pair, core, *grad_parts, out_weight, 1)
    pre = scatter_row(pre, z, {2: (back,)})
    lifted = jax.nn.relu(pre)
    pieces = gather_row((lifted * lifted).astype(BF16), z)
    back = scatter_row(after(back, pieces[ROWS - 2], pieces[ROWS]), z)
    hidden_grad = (back * (2.0 * lifted)).astype(BF16)

    hidden = spread(pair, info, pieces, height, hidden_local)
    out_term = y_parts(contract(hidden, all_grad, 0, 0))
    first = ring_first(out_term, y, *Y_RING)
    pieces = gather_row(hidden_grad, z, {2: (out_term,), 3: first})
    second = ring_second(out_term, y, *Y_RING, first)
    pieces[0] = after(pieces[0], *second)
    hidden_grad = spread(pair, info, pieces, height, hidden_local)
    in_terms = [
        y_parts(contract(hidden_grad, cols, 0, 0))
        for cols in (all_tokens[:, :width], all_tokens[:, width:])
    ]
    out_part = after(add(pick(out_term, y), *second), *in_terms)
    out_weight_grad = scatter_half(out_part, half, scale)
    in_weight_grad = jnp.concatenate(
        [scatter_half(scatter_ring(term, y, *Y_RING), half, scale) for term in in_terms], axis=1
    )
    hidden_grad = after(hidden_grad, *in_terms)
    token_grad = scatter_col(contract(hidden_grad, in_weight, 1, 1), x, core)
    return (token_grad, in_weight_grad, out_weight_grad)


def body(tokens, out_grad, in_weight, out_weight, active_lists, active_counts):
    col = lax.axis_index("col")
    local_blocks = in_weight.shape[1] // BLK
    active = active_pairs(active_lists, active_counts, local_blocks * lax.axis_size("col"))
    most = most_pairs(active, local_blocks)
    active = lax.dynamic_slice_in_dim(active, col * local_blocks, local_blocks, 1)
    ring = gather_x(tokens)
    most, out_grad = together(most, out_grad, *ring[1:])[:2]
    grad_ring = gather_x(out_grad)
    most = jnp.maximum(most, lax.ppermute(most, "dp", HALF_SWAP))
    token_parts = gather_core(ring, col // 2)
    grad_parts = gather_core((after(grad_ring[0], most), *grad_ring[1:]), col // 2)
    most = most[0, 0]
    fits = sum((most > capacity).astype(jnp.int32) for capacity in CAPACITIES)
    branches = [
        functools.partial(run, capacity) for capacity in (*CAPACITIES, active.shape[0] * local_blocks)
    ]
    return lax.switch(fits, branches, token_parts, grad_parts, in_weight, out_weight, active)


def solution(mesh):
    in_specs = (
        P(("dp", "col"), "row"),
        P(("dp", "col"), "row"),
        P("row", "col"),
        P("col", "row"),
        P("dp", None),
        P("dp"),
    )
    out_specs = (P(("dp", "col"), "row"), P(("col", "dp"), "row"), P(("col", "dp"), "row"))
    return jax.shard_map(body, mesh=mesh, in_specs=in_specs, out_specs=out_specs, check_vma=False)
```
